512 devices in a mesh: dp: 128 (over z, x, core), mp: 4 (over y).
Axes of the slice: x: 4, y: 4, z: 16, core: 2. Of those that a mesh axis runs over, the one named last changes fastest.
Arguments:
- query_states: bfloat16 [16384, 1024], P('dp'), may hold values from -41 to 41
- passage_states: bfloat16 [16384, 1024], P('dp'), may hold values from -41 to 41
- w_in: bfloat16 [1024, 4096], P(None, 'mp'), may hold values from -0.1875 to 0.1875
- w_out: bfloat16 [4096, 1024], P('mp'), may hold values from -0.09375 to 0.09375
- neg_owner: int32 [16384, 8], P('dp'), may hold values from 0 to 127, all different within a row; in each aligned block of 128 rows (0 to 127, 128 to 255, ...) at most 16 rows name the same one
- neg_mask: int32 [16384, 8], P('dp'), may hold values 0 or 1
- served_rows: int32 [128, 128, 16], P('dp'), may hold values from 0 to 127
- loss_scale: float32 [], replicated, may hold values from 32 to 128
Outputs:
- grad_query_states: bfloat16 [16384, 1024], P('dp', 'mp')
- grad_passage_states: bfloat16 [16384, 1024], P('dp', 'mp')
The draws below stay inside these ranges and needn't reach their ends.
Inputs may be any that keep to these rules, and one draw needn't show every extreme that they name: Within the queries of one owner (aligned blocks of 128 rows) no owner is named by more than 16 entries of neg_owner, and in some block one owner is named exactly 16 times; the 8 owners of one query are distinct.
All inputs are finite; a program needn't handle non-finite values. No bound on the sum of `neg_mask` on one device may be relied on, other than what follows from the above.
Results may differ from the reference program's by a relative error of at most 0.017.
Values may be sent and summed in bfloat16 or wider, within the bound.
A program may use at most 64 MiB of HBM per device.

```python
import math
import jax
import jax.numpy as jnp
import numpy as np
from jax import lax

D = 1024
FF = 4096
NEG = 8
Q_DEV = 128
CAP = 16
QUERIES = 16384
PASSAGES = 16384
N_DP = 128


def state_draw(key, row_total, salt):
    keys = jax.random.split(jax.random.fold_in(key, salt), 3)
    base = jnp.clip(jax.random.normal(keys[0], (row_total, D), jnp.float32), -4.0, 4.0)
    span = math.log(10.0)
    row_scale = jnp.exp(jax.random.uniform(keys[1], (row_total, 1), jnp.float32, 0.0, span) - 0.5 * span)
    column_scale = jnp.exp(jax.random.uniform(keys[2], (1, D), jnp.float32, 0.0, span) - 0.5 * span)
    return base * row_scale * column_scale


def draw_query_states(key, part):
    return state_draw(key, QUERIES, 101).astype(jnp.bfloat16)


def draw_passage_states(key, part):
    return state_draw(key, PASSAGES, 202).astype(jnp.bfloat16)


def plant(result, key, low, high):
    longest = result.shape.index(max(result.shape))
    spots = []
    for shift in (0, 1):
        where = [jax.random.randint(jax.random.fold_in(key, axis), (), 0, length) for axis, length in enumerate(result.shape)]
        where[longest] = (where[longest] + shift) % result.shape[longest]
        spots.append(tuple(where))
    return result.at[spots[0]].set(low).at[spots[1]].set(high)


def level_of(own_key, dims, pieces, least, high):
    loudness, own = 1.0, jax.random.fold_in(own_key, 6)
    for axis_at, shards_of in pieces:
        heights = jnp.exp(jax.random.uniform(jax.random.fold_in(own, axis_at), (shards_of,), jnp.float32, least / len(pieces), high / len(pieces)))
        loudness = loudness * jnp.repeat(heights, dims[axis_at] // shards_of).reshape([-1 if axis == axis_at else 1 for axis in range(len(dims))])
    return loudness


def routed_block(own_key, own, number, rows, amount, top, most, skew):
    sequence = jax.random.permutation(own_key, amount)
    crowded, usual = load_shares(amount, rows * top, most, skew, True), load_shares(amount, rows * top, most, skew, False)
    places = jnp.arange(amount)

    def named(sizes, rotation):
        used = int((sizes > 0).sum())
        fixed = max(1, used // 4)
        shifted = fixed + (places - fixed + rotation * (used - fixed)) % max(1, amount - fixed)
        return jnp.zeros((amount,), jnp.int32).at[sequence[jnp.where(places < fixed, places, shifted)]].set(jnp.asarray(sizes, jnp.int32))

    sizes = jnp.where(number % 4 == 0, named(crowded, number // 4), named(usual, number - number // 4 - 1))
    mixed = jax.random.permutation(jax.random.fold_in(own, 3), amount)
    source_of, taker = mixed[0:amount // 2 * 2:2], mixed[1:amount // 2 * 2:2]
    margin = jnp.minimum(sizes[source_of] - 1, most - sizes[taker]) // 2
    margin = jnp.where((source_of == sequence[0]) | (taker == sequence[0]) | (sizes[taker] == 0), 0, jnp.maximum(margin, 0))
    shifted = jax.random.randint(jax.random.fold_in(own, 4), (amount // 2,), 0, 1 << 20) % (margin + 1)
    sizes = sizes.at[source_of].add(-shifted).at[taker].add(shifted)
    labels = jnp.searchsorted(jnp.cumsum(sizes), jnp.arange(rows * top), side="right").astype(jnp.int32)
    listing = labels.reshape(top, rows).T
    listing = listing[jax.random.permutation(jax.random.fold_in(own, 1), rows)]
    rotation = jax.random.randint(jax.random.fold_in(own, 2), (rows, 1), 0, top)
    return jnp.take_along_axis(listing, (jnp.arange(top)[None, :] + rotation) % top, axis=1)


def load_shares(count, total, most, lean, full):
    portions = [(1 << 20) // math.isqrt(rank ** lean) + 1 for rank in range(1, count + 1)]
    largest = most if full else min(most, max(-(-total // count), total * portions[0] // sum(portions)))
    least = 1 if total - largest >= count - 1 else 0
    holding, rest = [largest] + [least] * (count - 1), total - largest - least * (count - 1)
    while rest > 0:
        movable = [i for i in range(1, count) if holding[i] < largest] or [i for i in range(1, count) if holding[i] < most]
        pool, budget = sum([portions[i] for i in movable]), rest
        for i in movable:
            addition = min(most - holding[i], max(1, budget * portions[i] // pool), rest)
            holding[i] = holding[i] + addition
            rest = rest - addition
    return np.array(holding)


def normal_values(own_key, shape, scale, bound, cuts=(), held_as=jnp.bfloat16):
    loudness = level_of(own_key, shape, cuts, -0.22, 0.18) if cuts else 1.0
    array = jax.random.normal(own_key, shape, jnp.float32) * scale * loudness
    return jnp.minimum(jnp.maximum(array, -bound), bound).astype(held_as)


def setup_inputs(seed: int = 0) -> dict:
    key_list = jax.random.split(jax.random.key(seed), 9)
    query_states = draw_query_states(jax.random.fold_in(key_list[8], 71), 0)
    passage_states = draw_passage_states(jax.random.fold_in(key_list[8], 71), 0)
    w_in = normal_values(key_list[2], (D, FF), D ** -0.5, 0.1875, ((1, 4),))
    w_out = normal_values(key_list[3], (FF, D), FF ** -0.5, 0.09375, ((0, 4),))
    neg_owner_keys = jax.random.split(jax.random.fold_in(key_list[4], 1), QUERIES // Q_DEV)
    neg_owner_turns = jax.random.permutation(jax.random.fold_in(key_list[4], 3), QUERIES // Q_DEV)
    neg_owner = jax.vmap(lambda own, number: routed_block(jax.random.fold_in(key_list[4], 2), own, number, Q_DEV, N_DP, NEG, CAP, 2))(neg_owner_keys, neg_owner_turns).reshape((QUERIES, NEG))
    neg_mask = plant((jax.random.randint(key_list[5], (QUERIES, NEG), 0, 4) < 3).astype(jnp.int32), jax.random.fold_in(key_list[5], 1), 0, 1)
    served_rows = plant(jax.random.randint(key_list[6], (N_DP, N_DP, CAP), 0, Q_DEV), jax.random.fold_in(key_list[6], 1), 0, Q_DEV - 1).astype(jnp.int32)
    loss_scale = jnp.clip(jnp.exp(jax.random.uniform(key_list[7], (), jnp.float32, math.log(32.0), math.log(128.0))), 32.0, 128.0)
    return dict(query_states=query_states, passage_states=passage_states, w_in=w_in, w_out=w_out, neg_owner=neg_owner, neg_mask=neg_mask, served_rows=served_rows, loss_scale=loss_scale)


logit_scale = 50.0
norm_eps = 1e-06
root_half = 0.7071067811865476
inv_root_two_pi = 0.3989422804014327

def gelu_value(values):
    return 0.5 * values * (1.0 + lax.erf(values * root_half))

def gelu_slope(values):
    return 0.5 * (1.0 + lax.erf(values * root_half)) + values * jnp.exp(-0.5 * values * values) * inv_root_two_pi

def encode(states, w_in, w_out):
    pre_act = jnp.dot(states, w_in, preferred_element_type=jnp.float32)
    hidden = gelu_value(pre_act).astype(jnp.bfloat16)
    output = states.astype(jnp.float32) + jnp.dot(hidden, w_out, preferred_element_type=jnp.float32)
    inv_norm = lax.rsqrt(lax.optimization_barrier(jnp.sum(output * output, axis=1, keepdims=True)) + norm_eps)
    return (pre_act, output * inv_norm, inv_norm)

def decode(grad_emb, pre_act, unit_rows, inv_norm, w_in, w_out):
    grad_out = inv_norm * (grad_emb - unit_rows * lax.optimization_barrier(jnp.sum(unit_rows * grad_emb, axis=1, keepdims=True)))
    grad_hidden = jnp.dot(grad_out.astype(jnp.bfloat16), w_out.T, preferred_element_type=jnp.float32)
    grad_pre = (grad_hidden * gelu_slope(pre_act)).astype(jnp.bfloat16)
    return (grad_out + jnp.dot(grad_pre, w_in.T, preferred_element_type=jnp.float32)).astype(jnp.bfloat16)

def reference(query_states, passage_states, w_in, w_out, neg_owner, neg_mask, served_rows, loss_scale):
    pre_query, unit_query, inv_query = encode(query_states, w_in, w_out)
    pre_pass, unit_pass, inv_pass = encode(passage_states, w_in, w_out)
    emb_query = unit_query.astype(jnp.bfloat16).astype(jnp.float32)
    emb_pass = unit_pass.astype(jnp.bfloat16).astype(jnp.float32)
    owner_block = neg_owner.reshape(N_DP, Q_DEV * NEG)
    onehot = (owner_block[:, :, None] == jnp.arange(N_DP, dtype=jnp.int32)[None, None, :]).astype(jnp.int32)
    before = jnp.cumsum(onehot, axis=1, dtype=jnp.int32) - onehot
    slot_index = lax.optimization_barrier(jnp.sum(before * onehot, axis=2, dtype=jnp.int32)).astype(jnp.int32)
    source = jnp.broadcast_to(jnp.arange(N_DP, dtype=jnp.int32)[:, None], owner_block.shape)
    neg_rows = served_rows[owner_block, source, slot_index].astype(jnp.int32)
    neg_id = (owner_block * Q_DEV + neg_rows).reshape(QUERIES, NEG).astype(jnp.int32)
    neg_emb = emb_pass[neg_id]
    pos_score = lax.optimization_barrier(jnp.sum(emb_query * emb_pass, axis=1))
    neg_score = lax.optimization_barrier(jnp.sum(emb_query[:, None, :] * neg_emb, axis=2))
    exp_pos = jnp.exp(logit_scale * pos_score)
    exp_neg = neg_mask.astype(jnp.float32) * jnp.exp(logit_scale * neg_score)
    denominator = exp_pos + lax.optimization_barrier(jnp.sum(exp_neg, axis=1))
    factor = loss_scale * logit_scale
    grad_pos = factor * (exp_pos / denominator - 1.0)
    grad_neg = factor * exp_neg / denominator[:, None]
    grad_query_emb = grad_pos[:, None] * emb_pass + lax.optimization_barrier(jnp.sum(grad_neg[:, :, None] * neg_emb, axis=1))
    slot_terms = (grad_neg[:, :, None] * emb_query[:, None, :]).astype(jnp.bfloat16).astype(jnp.float32)
    returned = jax.ops.segment_sum(slot_terms.reshape(QUERIES * NEG, D), neg_id.reshape(-1), num_segments=PASSAGES)
    grad_pass_emb = grad_pos[:, None] * emb_query + returned
    grad_query_states = decode(grad_query_emb, pre_query, unit_query, inv_query, w_in, w_out)
    grad_passage_states = decode(grad_pass_emb, pre_pass, unit_pass, inv_pass, w_in, w_out)
    return (grad_query_states, grad_passage_states)
```

```python
import jax
import jax.numpy as jnp
from jax import lax
from jax.sharding import PartitionSpec as P

logit_scale = 50.0
norm_eps = 1e-06
root_half = 0.7071067811865476
inv_root_two_pi = 0.3989422804014327


def gelu_value(values):
    return 0.5 * values * (1.0 + lax.erf(values * root_half))


def gelu_slope(values):
    return (
        0.5 * (1.0 + lax.erf(values * root_half))
        + values * jnp.exp(-0.5 * values * values) * inv_root_two_pi
    )


def own_columns(values):
    column_width = values.shape[1] // lax.axis_size("mp")
    return lax.dynamic_slice_in_dim(values, lax.axis_index("mp") * column_width, column_width, 1)


def encode(states, w_in, w_out):
    pre_act = jnp.dot(states, w_in, preferred_element_type=jnp.float32)
    hidden = gelu_value(pre_act).astype(jnp.bfloat16)
    partial_out = jnp.dot(hidden, w_out, preferred_element_type=jnp.float32)
    mixed_sum = lax.psum(partial_out, "mp")
    output = states.astype(jnp.float32) + mixed_sum
    inv_norm = lax.rsqrt(jnp.sum(output * output, axis=1, keepdims=True) + norm_eps)
    return (pre_act, output * inv_norm, inv_norm)


def decode(grad_part, pre_act, unit_rows, inv_norm, w_in, w_out):
    grad_emb = lax.all_gather(grad_part.astype(jnp.bfloat16), "mp", axis=1, tiled=True).astype(
        grad_part.dtype
    )
    grad_out = inv_norm * (
        grad_emb - unit_rows * jnp.sum(unit_rows * grad_emb, axis=1, keepdims=True)
    )
    contract = (((1,), (1,)), ((), ()))
    grad_hidden = lax.dot_general(
        grad_out.astype(jnp.bfloat16), w_out, contract, preferred_element_type=jnp.float32
    )
    grad_pre = (grad_hidden * gelu_slope(pre_act)).astype(jnp.bfloat16)
    partial_in = lax.dot_general(grad_pre, w_in, contract, preferred_element_type=jnp.float32)
    summed = lax.psum_scatter(
        partial_in.astype(jnp.bfloat16), "mp", scatter_dimension=1, tiled=True
    ).astype(jnp.float32)
    return (summed + own_columns(grad_out)).astype(jnp.bfloat16)


def shards(query_states, passage_states, w_in, w_out, neg_owner, neg_mask, served_rows, loss_scale):
    owners = lax.axis_size("dp")
    row_count = query_states.shape[0]
    negatives = neg_owner.shape[1]
    capacity = served_rows.shape[2]
    pre_pass, unit_pass, inv_pass = encode(passage_states, w_in, w_out)
    emb_pass = own_columns(unit_pass).astype(jnp.bfloat16)
    column_width = emb_pass.shape[1]
    slots = owners * capacity
    served = served_rows[0].reshape(-1)
    served_pick = (served[:, None] == jnp.arange(row_count, dtype=jnp.int32)[None, :]).astype(jnp.bfloat16)
    flat_owner = neg_owner.reshape(-1)
    onehot = (flat_owner[:, None] == jnp.arange(owners, dtype=jnp.int32)[None, :]).astype(jnp.int32)
    before = jnp.cumsum(onehot, axis=0, dtype=jnp.int32) - onehot
    slot_index = jnp.sum(before * onehot, axis=1, dtype=jnp.int32)
    slot_place = (flat_owner * capacity + slot_index).reshape(row_count, negatives)
    outgoing_emb = jnp.dot(served_pick, emb_pass, preferred_element_type=jnp.float32).astype(jnp.bfloat16)
    slot_emb = lax.all_to_all(
        outgoing_emb.reshape(owners, capacity, column_width), "dp", split_axis=0, concat_axis=0, tiled=True
    ).reshape(slots, column_width)
    slot_hit = slot_place[:, :, None] == jnp.arange(slots, dtype=jnp.int32)[None, None, :]
    pre_query, unit_query, inv_query = encode(query_states, w_in, w_out)
    emb_query = own_columns(unit_query).astype(jnp.bfloat16)
    pos_part = jnp.einsum("qd,qd->q", emb_query, emb_pass, preferred_element_type=jnp.float32)
    slot_part = lax.dot_general(emb_query, slot_emb, (((1,), (1,)), ((), ())), preferred_element_type=jnp.float32)
    neg_part = jnp.sum(jnp.where(slot_hit, slot_part[:, None, :], 0.0), axis=2)
    pos_score, neg_score = lax.psum((pos_part, neg_part), "mp")
    exp_pos = jnp.exp(logit_scale * pos_score)
    exp_neg = neg_mask.astype(jnp.float32) * jnp.exp(logit_scale * neg_score)
    denominator = exp_pos + jnp.sum(exp_neg, axis=1)
    factor = loss_scale * logit_scale
    grad_pos = factor * (exp_pos / denominator - 1.0)
    grad_neg = factor * exp_neg / denominator[:, None]
    query_values = emb_query.astype(jnp.float32)
    slot_grad = jnp.sum(jnp.where(slot_hit, grad_neg[:, :, None], 0.0), axis=1).astype(jnp.bfloat16)
    grad_query_emb = grad_pos[:, None] * emb_pass.astype(jnp.float32) + jnp.dot(
        slot_grad, slot_emb, preferred_element_type=jnp.float32
    )
    outgoing_grad = lax.dot_general(
        slot_grad, emb_query, (((0,), (0,)), ((), ())), preferred_element_type=jnp.float32
    ).astype(jnp.bfloat16)
    returned = lax.all_to_all(
        outgoing_grad.reshape(owners, capacity, column_width), "dp", split_axis=0, concat_axis=0, tiled=True
    ).reshape(slots, column_width)
    grad_query_states = decode(grad_query_emb, pre_query, unit_query, inv_query, w_in, w_out)
    gathered_back = lax.dot_general(
        served_pick, returned, (((0,), (0,)), ((), ())), preferred_element_type=jnp.float32
    )
    grad_pass_emb = grad_pos[:, None] * query_values + gathered_back
    grad_passage_states = decode(grad_pass_emb, pre_pass, unit_pass, inv_pass, w_in, w_out)
    return (grad_query_states, grad_passage_states)


def solution(mesh):
    in_specs = (
        P("dp", None),
        P("dp", None),
        P(None, "mp"),
        P("mp", None),
        P("dp", None),
        P("dp", None),
        P("dp", None, None),
        P(),
    )
    out_specs = (P("dp", "mp"), P("dp", "mp"))
    return jax.shard_map(shards, mesh=mesh, in_specs=in_specs, out_specs=out_specs, check_vma=False)
```

```python
import functools
import jax
import jax.numpy as jnp
from jax import lax
from jax.experimental import pallas as pl
from jax.experimental.pallas import tpu as pltpu
from jax.sharding import PartitionSpec as P

logit_scale = 50.0
norm_eps = 1e-06
root_half = 0.7071067811865476
inv_root_two_pi = 0.3989422804014327


def gelu_value(values):
    return 0.5 * values * (1.0 + lax.erf(values * root_half))


def gelu_slope(values):
    return (
        0.5 * (1.0 + lax.erf(values * root_half))
        + values * jnp.exp(-0.5 * values * values) * inv_root_two_pi
    )


def own_columns(values):
    column_width = values.shape[1] // lax.axis_size("mp")
    return lax.dynamic_slice_in_dim(values, lax.axis_index("mp") * column_width, column_width, 1)


def greet(ways):
    me = lax.axis_index("mp")
    barrier = pltpu.get_barrier_semaphore()
    for step in range(1, ways):
        pl.semaphore_signal(
            barrier, inc=1, device_id={"mp": lax.rem(me + step, ways)}, device_id_type=pl.DeviceIdType.MESH
        )
    pl.semaphore_wait(barrier, ways - 1)
    return me


def remote(source, target, send_sem, recv_sem, peer):
    return pltpu.make_async_remote_copy(
        src_ref=source,
        dst_ref=target,
        send_sem=send_sem,
        recv_sem=recv_sem,
        device_id={"mp": peer},
        device_id_type=pl.DeviceIdType.MESH,
    )


def block_of(ref, place, width):
    return ref.at[:, pl.ds(pl.multiple_of(place * width, 128), width)]


def scatter_kernel(ways, part_ref, out_ref, landed, send_sem, recv_sem):
    width = out_ref.shape[1]
    me = greet(ways)
    copies = []
    for step in range(1, ways):
        peer = lax.rem(me + step, ways)
        copy = remote(
            block_of(part_ref, peer, width),
            landed.at[step - 1],
            send_sem.at[step - 1],
            recv_sem.at[step - 1],
            peer,
        )
        copy.start()
        copies.append(copy)
    for copy in copies:
        copy.wait()
    own = part_ref[:, pl.ds(pl.multiple_of(me * width, 128), width)]
    total = own.astype(jnp.float32)
    for step in range(1, ways):
        total = total + landed[step - 1].astype(jnp.float32)
    out_ref[...] = total


def gather_kernel(ways, own_ref, out_ref, send_sem, recv_sem):
    width = own_ref.shape[1]
    me = greet(ways)
    copies = []
    for step in range(1, ways):
        copy = remote(
            own_ref,
            block_of(out_ref, me, width),
            send_sem.at[step - 1],
            recv_sem.at[step - 1],
            lax.rem(me + step, ways),
        )
        copy.start()
        copies.append(copy)
    out_ref[:, pl.ds(pl.multiple_of(me * width, 128), width)] = own_ref[...]
    for copy in copies:
        copy.wait()


def gather_sum_kernel(ways, own_ref, term_ref, out_ref, sum_ref, landed, send_sem, recv_sem, term_send, term_recv):
    width = own_ref.shape[1]
    me = greet(ways)
    copies = []
    for step in range(1, ways):
        peer = lax.rem(me + step, ways)
        term_copy = remote(
            term_ref, landed.at[step - 1], term_send.at[step - 1], term_recv.at[step - 1], peer
        )
        copy = remote(
            own_ref, block_of(out_ref, me, width), send_sem.at[step - 1], recv_sem.at[step - 1], peer
        )
        copy.start()
        term_copy.start()
        copies += [copy, term_copy]
    out_ref[:, pl.ds(pl.multiple_of(me * width, 128), width)] = own_ref[...]
    for copy in copies:
        copy.wait()
    total = term_ref[...]
    for step in range(1, ways):
        total = total + landed[step - 1]
    sum_ref[...] = total


def sum_kernel(ways, term_ref, sum_ref, landed, send_sem, recv_sem):
    me = greet(ways)
    copies = []
    for step in range(1, ways):
        copy = remote(
            term_ref,
            landed.at[step - 1],
            send_sem.at[step - 1],
            recv_sem.at[step - 1],
            lax.rem(me + step, ways),
        )
        copy.start()
        copies.append(copy)
    for copy in copies:
        copy.wait()
    total = term_ref[...]
    for step in range(1, ways):
        total = total + landed[step - 1]
    sum_ref[...] = total


def in_vmem(count):
    return [pl.BlockSpec(memory_space=pltpu.VMEM)] * count


def params(number):
    return pltpu.CompilerParams(collective_id=number, has_side_effects=True, vmem_limit_bytes=16 << 20)


def sems(ways):
    return [pltpu.SemaphoreType.DMA((ways - 1,)), pltpu.SemaphoreType.DMA((ways - 1,))]


def mp_scatter(part, number):
    ways = lax.axis_size("mp")
    rows, width = part.shape[0], part.shape[1] // ways
    return pl.pallas_call(
        functools.partial(scatter_kernel, ways),
        out_shape=jax.ShapeDtypeStruct((rows, width), jnp.float32),
        in_specs=in_vmem(1),
        out_specs=pl.BlockSpec(memory_space=pltpu.VMEM),
        scratch_shapes=[pltpu.VMEM((ways - 1, rows, width), part.dtype)] + sems(ways),
        compiler_params=params(number),
        cost_estimate=pl.CostEstimate(flops=rows * width * 4, bytes_accessed=part.size * 4, transcendentals=0),
        name="mp_scatter",
    )(part)


def mp_gather(own, number):
    ways = lax.axis_size("mp")
    rows, width = own.shape
    return pl.pallas_call(
        functools.partial(gather_kernel, ways),
        out_shape=jax.ShapeDtypeStruct((rows, ways * width), own.dtype),
        in_specs=in_vmem(1),
        out_specs=pl.BlockSpec(memory_space=pltpu.VMEM),
        scratch_shapes=sems(ways),
        compiler_params=params(number),
        cost_estimate=pl.CostEstimate(flops=0, bytes_accessed=own.size * 10, transcendentals=0),
        name="mp_gather",
    )(own)


def mp_gather_sum(own, term, number):
    ways = lax.axis_size("mp")
    rows, width = own.shape
    return pl.pallas_call(
        functools.partial(gather_sum_kernel, ways),
        out_shape=(
            jax.ShapeDtypeStruct((rows, ways * width), own.dtype),
            jax.ShapeDtypeStruct(term.shape, term.dtype),
        ),
        in_specs=in_vmem(2),
        out_specs=tuple(in_vmem(2)),
        scratch_shapes=[pltpu.VMEM((ways - 1,) + term.shape, term.dtype)] + sems(ways) + sems(ways),
        compiler_params=params(number),
        cost_estimate=pl.CostEstimate(flops=0, bytes_accessed=own.size * 10, transcendentals=0),
        name="mp_gather_sum",
    )(own, term)


def mp_sum(term, number):
    ways = lax.axis_size("mp")
    return pl.pallas_call(
        functools.partial(sum_kernel, ways),
        out_shape=jax.ShapeDtypeStruct(term.shape, term.dtype),
        in_specs=in_vmem(1),
        out_specs=pl.BlockSpec(memory_space=pltpu.VMEM),
        scratch_shapes=[pltpu.VMEM((ways - 1,) + term.shape, term.dtype)] + sems(ways),
        compiler_params=params(number),
        cost_estimate=pl.CostEstimate(flops=0, bytes_accessed=term.size * 20, transcendentals=0),
        name="mp_sum",
    )(term)


def decode(grad_own, pre_act, out_own, out_full, inv_norm, w_in, w_out, number):
    inv = inv_norm[:, None]
    unit_own = out_own * inv
    dot_part = jnp.sum(unit_own * grad_own, axis=1)
    grad_full, dots = mp_gather_sum(
        grad_own.astype(jnp.bfloat16), jnp.broadcast_to(dot_part[None, :], (8, dot_part.shape[0])), number
    )
    dot_all = dots[0][:, None]
    grad_out = inv * (grad_full.astype(jnp.float32) - out_full.astype(jnp.float32) * (inv * dot_all))
    grad_out_own = inv * (grad_own - unit_own * dot_all)
    contract = (((1,), (1,)), ((), ()))
    grad_hidden = lax.dot_general(
        grad_out.astype(jnp.bfloat16), w_out, contract, preferred_element_type=jnp.float32
    )
    grad_pre = (grad_hidden * gelu_slope(pre_act)).astype(jnp.bfloat16)
    partial_in = lax.dot_general(grad_pre, w_in, contract, preferred_element_type=jnp.float32)
    summed = mp_scatter(partial_in.astype(jnp.bfloat16), number + 1)
    return (summed + grad_out_own).astype(jnp.bfloat16)


def shards(query_states, passage_states, w_in, w_out, neg_owner, neg_mask, served_rows, loss_scale):
    owners = lax.axis_size("dp")
    row_count = query_states.shape[0]
    capacity = served_rows.shape[2]
    slots = owners * capacity
    states = jnp.concatenate([passage_states, query_states], axis=0)
    pre_act = jnp.dot(states, w_in, preferred_element_type=jnp.float32)
    hidden = gelu_value(pre_act).astype(jnp.bfloat16)
    partial_out = jnp.dot(hidden, w_out, preferred_element_type=jnp.float32).astype(jnp.bfloat16)
    out_own = own_columns(states).astype(jnp.float32) + mp_scatter(partial_out, 0)
    out_pass, out_query = out_own[:row_count], out_own[row_count:]
    out_half = out_own.astype(jnp.bfloat16)
    half_pass, half_query = out_half[:row_count], out_half[row_count:]
    column_width = half_pass.shape[1]

    served = served_rows[0].reshape(-1)
    served_pick = (served[:, None] == jnp.arange(row_count, dtype=jnp.int32)[None, :]).astype(jnp.bfloat16)
    flat_owner = neg_owner.reshape(-1)
    onehot = (flat_owner[:, None] == jnp.arange(owners, dtype=jnp.int32)[None, :]).astype(jnp.int32)
    before = jnp.cumsum(onehot, axis=0, dtype=jnp.int32) - onehot
    slot_index = jnp.sum(before * onehot, axis=1, dtype=jnp.int32)
    slot_place = (flat_owner * capacity + slot_index).reshape(neg_owner.shape).T
    outgoing_rows = jnp.dot(served_pick, half_pass, preferred_element_type=jnp.float32).astype(jnp.bfloat16)
    slot_rows = lax.all_to_all(
        outgoing_rows.reshape(owners, capacity, column_width), "dp", split_axis=0, concat_axis=0, tiled=True
    ).reshape(slots, column_width)
    out_full = mp_gather(out_half, 1)
    slot_hit = slot_place[:, :, None] == jnp.arange(slots, dtype=jnp.int32)[None, None, :]

    slot_part = lax.dot_general(half_query, slot_rows, (((1,), (1,)), ((), ())), preferred_element_type=jnp.float32)
    slot_wide = slot_rows.astype(jnp.float32)
    slot_square = jnp.sum(slot_wide * slot_wide, axis=1)
    neg_part = jnp.sum(jnp.where(slot_hit, slot_part[None, :, :], 0.0), axis=2)
    neg_square = jnp.sum(jnp.where(slot_hit, slot_square[None, None, :], 0.0), axis=2)
    pos_part = jnp.sum(half_query.astype(jnp.float32) * half_pass.astype(jnp.float32), axis=1)
    squares = jnp.sum(out_own * out_own, axis=1).reshape(2, row_count)
    extra = jnp.concatenate([pos_part[None, :], squares, jnp.zeros((5, row_count), jnp.float32)], axis=0)
    sums = mp_sum(jnp.concatenate([neg_part, neg_square, extra], axis=0), 2)
    negatives = neg_owner.shape[1]
    inv_neg = lax.rsqrt(sums[negatives : 2 * negatives] + norm_eps)
    inv_pass = lax.rsqrt(sums[2 * negatives + 1] + norm_eps)
    inv_query = lax.rsqrt(sums[2 * negatives + 2] + norm_eps)
    pos_score = sums[2 * negatives] * inv_query * inv_pass
    neg_score = sums[:negatives] * inv_query[None, :] * inv_neg
    exp_pos = jnp.exp(logit_scale * pos_score)
    exp_neg = neg_mask.T.astype(jnp.float32) * jnp.exp(logit_scale * neg_score)
    denominator = exp_pos + jnp.sum(exp_neg, axis=0)
    factor = loss_scale * logit_scale
    grad_pos = factor * (exp_pos / denominator - 1.0)
    grad_neg = factor * exp_neg / denominator[None, :]

    slot_grad = jnp.sum(jnp.where(slot_hit, (grad_neg * inv_query[None, :])[:, :, None], 0.0), axis=0)
    outgoing_grad = lax.dot_general(
        slot_grad.astype(jnp.bfloat16), half_query, (((0,), (0,)), ((), ())), preferred_element_type=jnp.float32
    ).astype(jnp.bfloat16)
    returned = lax.all_to_all(
        outgoing_grad.reshape(owners, capacity, column_width), "dp", split_axis=0, concat_axis=0, tiled=True
    ).reshape(slots, column_width)
    slot_weight = jnp.sum(jnp.where(slot_hit, (grad_neg * inv_neg)[:, :, None], 0.0), axis=0)
    grad_query_emb = (grad_pos * inv_pass)[:, None] * out_pass + jnp.dot(
        slot_weight.astype(jnp.bfloat16), slot_rows, preferred_element_type=jnp.float32
    )
    grad_query_states = decode(
        grad_query_emb, pre_act[row_count:], out_query, out_full[row_count:], inv_query, w_in, w_out, 3
    )
    returned, grad_query_states = lax.optimization_barrier((returned, grad_query_states))
    gathered_back = lax.dot_general(
        served_pick, returned, (((0,), (0,)), ((), ())), preferred_element_type=jnp.float32
    )
    grad_pass_emb = (grad_pos * inv_query)[:, None] * out_query + gathered_back
    grad_passage_states = decode(
        grad_pass_emb, pre_act[:row_count], out_pass, out_full[:row_count], inv_pass, w_in, w_out, 5
    )
    return (grad_query_states, grad_passage_states)


def solution(mesh):
    in_specs = (
        P("dp", None),
        P("dp", None),
        P(None, "mp"),
        P("mp", None),
        P("dp", None),
        P("dp", None),
        P("dp", None, None),
        P(),
    )
    out_specs = (P("dp", "mp"), P("dp", "mp"))
    return jax.shard_map(shards, mesh=mesh, in_specs=in_specs, out_specs=out_specs, check_vma=False)
```

```python
import functools
import jax
import jax.numpy as jnp
from jax import lax
from jax.experimental import pallas as pl
from jax.experimental.pallas import tpu as pltpu
from jax.sharding import PartitionSpec as P

logit_scale = 50.0
norm_eps = 1e-06
root_half = 0.7071067811865476
inv_root_two_pi = 0.3989422804014327


def gelu_value(values):
    return 0.5 * values * (1.0 + lax.erf(values * root_half))


def gelu_slope(values):
    return (
        0.5 * (1.0 + lax.erf(values * root_half))
        + values * jnp.exp(-0.5 * values * values) * inv_root_two_pi
    )


def own_columns(values):
    column_width = values.shape[1] // lax.axis_size("mp")
    return lax.dynamic_slice_in_dim(values, lax.axis_index("mp") * column_width, column_width, 1)


def greet(ways):
    me = lax.axis_index("mp")
    barrier = pltpu.get_barrier_semaphore()
    for step in range(1, ways):
        pl.semaphore_signal(
            barrier, inc=1, device_id={"mp": lax.rem(me + step, ways)}, device_id_type=pl.DeviceIdType.MESH
        )
    pl.semaphore_wait(barrier, ways - 1)
    return me


def remote(source, target, send_sem, recv_sem, peer):
    return pltpu.make_async_remote_copy(
        src_ref=source,
        dst_ref=target,
        send_sem=send_sem,
        recv_sem=recv_sem,
        device_id={"mp": peer},
        device_id_type=pl.DeviceIdType.MESH,
    )


def block_of(ref, place, width):
    return ref.at[:, pl.ds(pl.multiple_of(place * width, 128), width)]


def scatter_kernel(ways, part_ref, out_ref, landed, send_sem, recv_sem):
    width = out_ref.shape[1]
    me = greet(ways)
    copies = []
    for step in range(1, ways):
        peer = lax.rem(me + step, ways)
        copy = remote(
            block_of(part_ref, peer, width),
            landed.at[step - 1],
            send_sem.at[step - 1],
            recv_sem.at[step - 1],
            peer,
        )
        copy.start()
        copies.append(copy)
    for copy in copies:
        copy.wait()
    own = part_ref[:, pl.ds(pl.multiple_of(me * width, 128), width)]
    total = own.astype(jnp.float32)
    for step in range(1, ways):
        total = total + landed[step - 1].astype(jnp.float32)
    out_ref[...] = total


def gather_kernel(ways, own_ref, out_ref, send_sem, recv_sem):
    width = own_ref.shape[1]
    me = greet(ways)
    copies = []
    for step in range(1, ways):
        copy = remote(
            own_ref,
            block_of(out_ref, me, width),
            send_sem.at[step - 1],
            recv_sem.at[step - 1],
            lax.rem(me + step, ways),
        )
        copy.start()
        copies.append(copy)
    out_ref[:, pl.ds(pl.multiple_of(me * width, 128), width)] = own_ref[...]
    for copy in copies:
        copy.wait()


def gather_sum_kernel(ways, own_ref, term_ref, out_ref, sum_ref, landed, send_sem, recv_sem, term_send, term_recv):
    width = own_ref.shape[1]
    me = greet(ways)
    copies = []
    for step in range(1, ways):
        peer = lax.rem(me + step, ways)
        term_copy = remote(
            term_ref, landed.at[step - 1], term_send.at[step - 1], term_recv.at[step - 1], peer
        )
        copy = remote(
            own_ref, block_of(out_ref, me, width), send_sem.at[step - 1], recv_sem.at[step - 1], peer
        )
        copy.start()
        term_copy.start()
        copies += [copy, term_copy]
    out_ref[:, pl.ds(pl.multiple_of(me * width, 128), width)] = own_ref[...]
    for copy in copies:
        copy.wait()
    total = term_ref[...]
    for step in range(1, ways):
        total = total + landed[step - 1]
    sum_ref[...] = total


def sum_kernel(ways, term_ref, sum_ref, landed, send_sem, recv_sem):
    me = greet(ways)
    copies = []
    for step in range(1, ways):
        copy = remote(
            term_ref,
            landed.at[step - 1],
            send_sem.at[step - 1],
            recv_sem.at[step - 1],
            lax.rem(me + step, ways),
        )
        copy.start()
        copies.append(copy)
    for copy in copies:
        copy.wait()
    total = term_ref[...]
    for step in range(1, ways):
        total = total + landed[step - 1]
    sum_ref[...] = total


def in_vmem(count):
    return [pl.BlockSpec(memory_space=pltpu.VMEM)] * count


def params(number):
    return pltpu.CompilerParams(collective_id=number, has_side_effects=True, vmem_limit_bytes=16 << 20)


def sems(ways):
    return [pltpu.SemaphoreType.DMA((ways - 1,)), pltpu.SemaphoreType.DMA((ways - 1,))]


def mp_scatter(part, number):
    ways = lax.axis_size("mp")
    rows, width = part.shape[0], part.shape[1] // ways
    return pl.pallas_call(
        functools.partial(scatter_kernel, ways),
        out_shape=jax.ShapeDtypeStruct((rows, width), jnp.float32),
        in_specs=in_vmem(1),
        out_specs=pl.BlockSpec(memory_space=pltpu.VMEM),
        scratch_shapes=[pltpu.VMEM((ways - 1, rows, width), part.dtype)] + sems(ways),
        compiler_params=params(number),
        cost_estimate=pl.CostEstimate(flops=rows * width * 4, bytes_accessed=part.size * 4, transcendentals=0),
        name="mp_scatter",
    )(part)


def mp_gather(own, number):
    ways = lax.axis_size("mp")
    rows, width = own.shape
    return pl.pallas_call(
        functools.partial(gather_kernel, ways),
        out_shape=jax.ShapeDtypeStruct((rows, ways * width), own.dtype),
        in_specs=in_vmem(1),
        out_specs=pl.BlockSpec(memory_space=pltpu.VMEM),
        scratch_shapes=sems(ways),
        compiler_params=params(number),
        cost_estimate=pl.CostEstimate(flops=0, bytes_accessed=own.size * 10, transcendentals=0),
        name="mp_gather",
    )(own)


def mp_gather_sum(own, term, number):
    ways = lax.axis_size("mp")
    rows, width = own.shape
    return pl.pallas_call(
        functools.partial(gather_sum_kernel, ways),
        out_shape=(
            jax.ShapeDtypeStruct((rows, ways * width), own.dtype),
            jax.ShapeDtypeStruct(term.shape, term.dtype),
        ),
        in_specs=in_vmem(2),
        out_specs=tuple(in_vmem(2)),
        scratch_shapes=[pltpu.VMEM((ways - 1,) + term.shape, term.dtype)] + sems(ways) + sems(ways),
        compiler_params=params(number),
        cost_estimate=pl.CostEstimate(flops=0, bytes_accessed=own.size * 10, transcendentals=0),
        name="mp_gather_sum",
    )(own, term)


def mp_sum(term, number):
    ways = lax.axis_size("mp")
    return pl.pallas_call(
        functools.partial(sum_kernel, ways),
        out_shape=jax.ShapeDtypeStruct(term.shape, term.dtype),
        in_specs=in_vmem(1),
        out_specs=pl.BlockSpec(memory_space=pltpu.VMEM),
        scratch_shapes=[pltpu.VMEM((ways - 1,) + term.shape, term.dtype)] + sems(ways),
        compiler_params=params(number),
        cost_estimate=pl.CostEstimate(flops=0, bytes_accessed=term.size * 20, transcendentals=0),
        name="mp_sum",
    )(term)


def decode(grad_own, pre_act, out_own, out_full, inv_norm, w_in, w_out, number):
    inv = inv_norm[:, None]
    unit_own = out_own * inv
    dot_part = jnp.sum(unit_own * grad_own, axis=1)
    grad_full, dots = mp_gather_sum(
        grad_own.astype(jnp.bfloat16), jnp.broadcast_to(dot_part[None, :], (8, dot_part.shape[0])), number
    )
    dot_all = dots[0][:, None]
    grad_out = inv * (grad_full.astype(jnp.float32) - out_full.astype(jnp.float32) * (inv * dot_all))
    grad_out_own = inv * (grad_own - unit_own * dot_all)
    contract = (((1,), (1,)), ((), ()))
    grad_hidden = lax.dot_general(
        grad_out.astype(jnp.bfloat16), w_out, contract, preferred_element_type=jnp.float32
    )
    grad_pre = (grad_hidden * gelu_slope(pre_act)).astype(jnp.bfloat16)
    partial_in = lax.dot_general(grad_pre, w_in, contract, preferred_element_type=jnp.float32)
    summed = mp_scatter(partial_in.astype(jnp.bfloat16), number + 1)
    return (summed + grad_out_own).astype(jnp.bfloat16)


def encode(states, w_in, w_out, number):
    pre_act = jnp.dot(states, w_in, preferred_element_type=jnp.float32)
    hidden = gelu_value(pre_act).astype(jnp.bfloat16)
    partial_out = jnp.dot(hidden, w_out, preferred_element_type=jnp.float32).astype(jnp.bfloat16)
    return (pre_act, own_columns(states).astype(jnp.float32) + mp_scatter(partial_out, number))


def shards(query_states, passage_states, w_in, w_out, neg_owner, neg_mask, served_rows, loss_scale):
    owners = lax.axis_size("dp")
    row_count = query_states.shape[0]
    capacity = served_rows.shape[2]
    slots = owners * capacity
    pre_pass, out_pass = encode(passage_states, w_in, w_out, 0)
    half_pass = out_pass.astype(jnp.bfloat16)
    column_width = half_pass.shape[1]

    served = served_rows[0].reshape(-1)
    served_pick = (served[:, None] == jnp.arange(row_count, dtype=jnp.int32)[None, :]).astype(jnp.bfloat16)
    outgoing_rows = jnp.dot(served_pick, half_pass, preferred_element_type=jnp.float32).astype(jnp.bfloat16)
    query_states, outgoing_rows = lax.optimization_barrier((query_states, outgoing_rows))
    slot_rows = lax.all_to_all(
        outgoing_rows.reshape(owners, capacity, column_width), "dp", split_axis=0, concat_axis=0, tiled=True
    ).reshape(slots, column_width)
    pre_query, out_query = encode(query_states, w_in, w_out, 7)
    half_query = out_query.astype(jnp.bfloat16)
    out_full = mp_gather(jnp.concatenate([half_pass, half_query], axis=0), 1)
    owner_rows = neg_owner.T
    named = owner_rows[:, :, None] == jnp.arange(owners, dtype=jnp.int32)[None, None, :]
    names = jnp.any(named, axis=0).astype(jnp.bfloat16)
    spot = jnp.arange(row_count, dtype=jnp.int32)
    earlier = (spot[None, :] < spot[:, None]).astype(jnp.bfloat16)
    before = jnp.dot(earlier, names, preferred_element_type=jnp.float32)
    slot_index = jnp.sum(jnp.where(named, before[None, :, :], 0.0), axis=2).astype(jnp.int32)
    slot_place = owner_rows * capacity + slot_index
    slot_hit = slot_place[:, :, None] == jnp.arange(slots, dtype=jnp.int32)[None, None, :]

    slot_part = lax.dot_general(half_query, slot_rows, (((1,), (1,)), ((), ())), preferred_element_type=jnp.float32)
    slot_wide = slot_rows.astype(jnp.float32)
    slot_square = jnp.sum(slot_wide * slot_wide, axis=1)
    neg_part = jnp.sum(jnp.where(slot_hit, slot_part[None, :, :], 0.0), axis=2)
    neg_square = jnp.sum(jnp.where(slot_hit, slot_square[None, None, :], 0.0), axis=2)
    pos_part = jnp.sum(half_query.astype(jnp.float32) * half_pass.astype(jnp.float32), axis=1)
    squares = jnp.stack([jnp.sum(out_pass * out_pass, axis=1), jnp.sum(out_query * out_query, axis=1)])
    extra = jnp.concatenate([pos_part[None, :], squares, jnp.zeros((5, row_count), jnp.float32)], axis=0)
    sums = mp_sum(jnp.concatenate([neg_part, neg_square, extra], axis=0), 2)
    negatives = neg_owner.shape[1]
    inv_neg = lax.rsqrt(sums[negatives : 2 * negatives] + norm_eps)
    inv_pass = lax.rsqrt(sums[2 * negatives + 1] + norm_eps)
    inv_query = lax.rsqrt(sums[2 * negatives + 2] + norm_eps)
    pos_score = sums[2 * negatives] * inv_query * inv_pass
    neg_score = sums[:negatives] * inv_query[None, :] * inv_neg
    exp_pos = jnp.exp(logit_scale * pos_score)
    exp_neg = neg_mask.T.astype(jnp.float32) * jnp.exp(logit_scale * neg_score)
    denominator = exp_pos + jnp.sum(exp_neg, axis=0)
    factor = loss_scale * logit_scale
    grad_pos = factor * (exp_pos / denominator - 1.0)
    grad_neg = factor * exp_neg / denominator[None, :]

    slot_grad = jnp.sum(jnp.where(slot_hit, (grad_neg * inv_query[None, :])[:, :, None], 0.0), axis=0)
    outgoing_grad = lax.dot_general(
        slot_grad.astype(jnp.bfloat16), half_query, (((0,), (0,)), ((), ())), preferred_element_type=jnp.float32
    ).astype(jnp.bfloat16)
    returned = lax.all_to_all(
        outgoing_grad.reshape(owners, capacity, column_width), "dp", split_axis=0, concat_axis=0, tiled=True
    ).reshape(slots, column_width)
    slot_weight = jnp.sum(jnp.where(slot_hit, (grad_neg * inv_neg)[:, :, None], 0.0), axis=0)
    grad_query_emb = (grad_pos * inv_pass)[:, None] * out_pass + jnp.dot(
        slot_weight.astype(jnp.bfloat16), slot_rows, preferred_element_type=jnp.float32
    )
    grad_query_states = decode(
        grad_query_emb, pre_query, out_query, out_full[row_count:], inv_query, w_in, w_out, 3
    )
    returned, grad_query_states = lax.optimization_barrier((returned, grad_query_states))
    gathered_back = lax.dot_general(
        served_pick, returned, (((0,), (0,)), ((), ())), preferred_element_type=jnp.float32
    )
    grad_pass_emb = (grad_pos * inv_query)[:, None] * out_query + gathered_back
    grad_passage_states = decode(
        grad_pass_emb, pre_pass, out_pass, out_full[:row_count], inv_pass, w_in, w_out, 5
    )
    return (grad_query_states, grad_passage_states)


def solution(mesh):
    in_specs = (
        P("dp", None),
        P("dp", None),
        P(None, "mp"),
        P("mp", None),
        P("dp", None),
        P("dp", None),
        P("dp", None, None),
        P(),
    )
    out_specs = (P("dp", "mp"), P("dp", "mp"))
    return jax.shard_map(shards, mesh=mesh, in_specs=in_specs, out_specs=out_specs, check_vma=False)
```

```python
import functools
import jax
import jax.numpy as jnp
from jax import lax
from jax.experimental import pallas as pl
from jax.experimental.pallas import tpu as pltpu
from jax.sharding import PartitionSpec as P

logit_scale = 50.0
norm_eps = 1e-06
root_half = 0.7071067811865476
inv_root_two_pi = 0.3989422804014327


def gelu_value(values):
    return 0.5 * values * (1.0 + lax.erf(values * root_half))


def gelu_slope(values):
    return (
        0.5 * (1.0 + lax.erf(values * root_half))
        + values * jnp.exp(-0.5 * values * values) * inv_root_two_pi
    )


def own_columns(values):
    column_width = values.shape[1] // lax.axis_size("mp")
    return lax.dynamic_slice_in_dim(values, lax.axis_index("mp") * column_width, column_width, 1)


def greet(ways):
    me = lax.axis_index("mp")
    barrier = pltpu.get_barrier_semaphore()
    for step in range(1, ways):
        pl.semaphore_signal(
            barrier, inc=1, device_id={"mp": lax.rem(me + step, ways)}, device_id_type=pl.DeviceIdType.MESH
        )
    pl.semaphore_wait(barrier, ways - 1)
    return me


def remote(source, target, send_sem, recv_sem, peer):
    return pltpu.make_async_remote_copy(
        src_ref=source,
        dst_ref=target,
        send_sem=send_sem,
        recv_sem=recv_sem,
        device_id={"mp": peer},
        device_id_type=pl.DeviceIdType.MESH,
    )


def block_of(ref, place, width):
    return ref.at[:, pl.ds(pl.multiple_of(place * width, 128), width)]


def scatter_kernel(ways, part_ref, out_ref, landed, send_sem, recv_sem):
    width = out_ref.shape[1]
    me = greet(ways)
    copies = []
    for step in range(1, ways):
        peer = lax.rem(me + step, ways)
        copy = remote(
            block_of(part_ref, peer, width),
            landed.at[step - 1],
            send_sem.at[step - 1],
            recv_sem.at[step - 1],
            peer,
        )
        copy.start()
        copies.append(copy)
    for copy in copies:
        copy.wait()
    own = part_ref[:, pl.ds(pl.multiple_of(me * width, 128), width)]
    total = own.astype(jnp.float32)
    for step in range(1, ways):
        total = total + landed[step - 1].astype(jnp.float32)
    out_ref[...] = total


def gather_kernel(ways, own_ref, out_ref, send_sem, recv_sem):
    width = own_ref.shape[1]
    me = greet(ways)
    copies = []
    for step in range(1, ways):
        copy = remote(
            own_ref,
            block_of(out_ref, me, width),
            send_sem.at[step - 1],
            recv_sem.at[step - 1],
            lax.rem(me + step, ways),
        )
        copy.start()
        copies.append(copy)
    out_ref[:, pl.ds(pl.multiple_of(me * width, 128), width)] = own_ref[...]
    for copy in copies:
        copy.wait()


def gather_sum_kernel(ways, own_ref, term_ref, out_ref, sum_ref, landed, send_sem, recv_sem, term_send, term_recv):
    width = own_ref.shape[1]
    me = greet(ways)
    copies = []
    for step in range(1, ways):
        peer = lax.rem(me + step, ways)
        term_copy = remote(
            term_ref, landed.at[step - 1], term_send.at[step - 1], term_recv.at[step - 1], peer
        )
        copy = remote(
            own_ref, block_of(out_ref, me, width), send_sem.at[step - 1], recv_sem.at[step - 1], peer
        )
        copy.start()
        term_copy.start()
        copies += [copy, term_copy]
    out_ref[:, pl.ds(pl.multiple_of(me * width, 128), width)] = own_ref[...]
    for copy in copies:
        copy.wait()
    total = term_ref[...]
    for step in range(1, ways):
        total = total + landed[step - 1]
    sum_ref[...] = total


def sum_kernel(ways, term_ref, sum_ref, landed, send_sem, recv_sem):
    me = greet(ways)
    copies = []
    for step in range(1, ways):
        copy = remote(
            term_ref,
            landed.at[step - 1],
            send_sem.at[step - 1],
            recv_sem.at[step - 1],
            lax.rem(me + step, ways),
        )
        copy.start()
        copies.append(copy)
    for copy in copies:
        copy.wait()
    total = term_ref[...]
    for step in range(1, ways):
        total = total + landed[step - 1]
    sum_ref[...] = total


def column_kernel(ways, plane, parts, block_ref, part_ref, column_ref, out_ref, landed, mp_send, mp_recv, up_send, up_recv, down_send, down_recv):
    depth, rows = column_ref.shape[0], column_ref.shape[1]
    width = out_ref.shape[1]
    piece = rows // parts
    me, place = lax.axis_index("mp"), lax.axis_index("dp")
    count = depth * plane
    high, here = place // plane, lax.rem(place, plane)
    above = lax.rem(place + plane, count)
    below = lax.rem(place + count - plane, count)
    barrier = pltpu.get_barrier_semaphore()
    for step in range(1, ways):
        pl.semaphore_signal(
            barrier, inc=1, device_id={"mp": lax.rem(me + step, ways)}, device_id_type=pl.DeviceIdType.MESH
        )
    for neighbour in (above, below):
        pl.semaphore_signal(barrier, inc=1, device_id={"dp": neighbour}, device_id_type=pl.DeviceIdType.MESH)
    pl.semaphore_wait(barrier, ways + 1)

    def hop(step, part, upward):
        rank = lax.rem(high + depth - (step - 1), depth) if upward else lax.rem(high + step - 1, depth)
        span = pl.ds(part * piece, piece)
        target = column_ref.at[rank, span]
        return pltpu.make_async_remote_copy(
            src_ref=block_ref.at[span] if step == 1 else target,
            dst_ref=target,
            send_sem=(up_send if upward else down_send).at[(step - 1) * parts + part],
            recv_sem=(up_recv if upward else down_recv).at[(step - 1) * parts + part],
            device_id={"dp": above if upward else below},
            device_id_type=pl.DeviceIdType.MESH,
        )

    up_steps, down_steps = depth // 2, depth - 1 - depth // 2
    hops = {}
    for part in range(parts):
        for upward in (True, False):
            hops[1, part, upward] = hop(1, part, upward)
            hops[1, part, upward].start()
    copies = []
    for step in range(1, ways):
        peer = lax.rem(me + step, ways)
        copy = remote(
            block_of(part_ref, peer, width),
            landed.at[step - 1],
            mp_send.at[step - 1],
            mp_recv.at[step - 1],
            peer,
        )
        copy.start()
        copies.append(copy)
    column_ref[high] = block_ref[...]
    for step in range(2, up_steps + 1):
        for part in range(parts):
            for upward in (True, False):
                hops[step - 1, part, upward].wait_recv() if (step - 1, part, upward) in hops else None
                if upward or step <= down_steps:
                    hops[step, part, upward] = hop(step, part, upward)
                    hops[step, part, upward].start()
    for copy in copies:
        copy.wait()
    own = part_ref[:, pl.ds(pl.multiple_of(me * width, 128), width)]
    total = own.astype(jnp.float32)
    for step in range(1, ways):
        total = total + landed[step - 1].astype(jnp.float32)
    out_ref[...] = total
    for (step, part, upward), copy in hops.items():
        if step == up_steps:
            copy.wait_recv()
        copy.wait_send()


def plane_kernel(plane, capacity, rows_ref, out_ref, send_sem, recv_sem):
    place = lax.axis_index("dp")
    here = lax.rem(place, plane)
    base = place - here
    barrier = pltpu.get_barrier_semaphore()
    for step in range(1, plane):
        pl.semaphore_signal(
            barrier,
            inc=1,
            device_id={"dp": base + lax.rem(here + step, plane)},
            device_id_type=pl.DeviceIdType.MESH,
        )
    pl.semaphore_wait(barrier, plane - 1)
    own = pl.ds(pl.multiple_of(here * capacity, capacity), capacity)
    copies = []
    for step in range(1, plane):
        peer = lax.rem(here + step, plane)
        copy = pltpu.make_async_remote_copy(
            src_ref=rows_ref.at[:, pl.ds(pl.multiple_of(peer * capacity, capacity), capacity)],
            dst_ref=out_ref.at[:, own],
            send_sem=send_sem.at[step - 1],
            recv_sem=recv_sem.at[step - 1],
            device_id={"dp": base + peer},
            device_id_type=pl.DeviceIdType.MESH,
        )
        copy.start()
        copies.append(copy)
    out_ref[:, own] = rows_ref[:, own]
    for copy in copies:
        copy.wait()


def in_vmem(count):
    return [pl.BlockSpec(memory_space=pltpu.VMEM)] * count


def params(number):
    return pltpu.CompilerParams(collective_id=number, has_side_effects=True, vmem_limit_bytes=16 << 20)


def sems(ways):
    return [pltpu.SemaphoreType.DMA((ways - 1,)), pltpu.SemaphoreType.DMA((ways - 1,))]


def mp_scatter(part, number):
    ways = lax.axis_size("mp")
    rows, width = part.shape[0], part.shape[1] // ways
    return pl.pallas_call(
        functools.partial(scatter_kernel, ways),
        out_shape=jax.ShapeDtypeStruct((rows, width), jnp.float32),
        in_specs=in_vmem(1),
        out_specs=pl.BlockSpec(memory_space=pltpu.VMEM),
        scratch_shapes=[pltpu.VMEM((ways - 1, rows, width), part.dtype)] + sems(ways),
        compiler_params=params(number),
        cost_estimate=pl.CostEstimate(flops=rows * width * 4, bytes_accessed=part.size * 4, transcendentals=0),
        name="mp_scatter",
    )(part)


def mp_gather(own, number):
    ways = lax.axis_size("mp")
    rows, width = own.shape
    return pl.pallas_call(
        functools.partial(gather_kernel, ways),
        out_shape=jax.ShapeDtypeStruct((rows, ways * width), own.dtype),
        in_specs=in_vmem(1),
        out_specs=pl.BlockSpec(memory_space=pltpu.VMEM),
        scratch_shapes=sems(ways),
        compiler_params=params(number),
        cost_estimate=pl.CostEstimate(flops=0, bytes_accessed=own.size * 10, transcendentals=0),
        name="mp_gather",
    )(own)


def mp_gather_sum(own, term, number):
    ways = lax.axis_size("mp")
    rows, width = own.shape
    return pl.pallas_call(
        functools.partial(gather_sum_kernel, ways),
        out_shape=(
            jax.ShapeDtypeStruct((rows, ways * width), own.dtype),
            jax.ShapeDtypeStruct(term.shape, term.dtype),
        ),
        in_specs=in_vmem(2),
        out_specs=tuple(in_vmem(2)),
        scratch_shapes=[pltpu.VMEM((ways - 1,) + term.shape, term.dtype)] + sems(ways) + sems(ways),
        compiler_params=params(number),
        cost_estimate=pl.CostEstimate(flops=0, bytes_accessed=own.size * 10, transcendentals=0),
        name="mp_gather_sum",
    )(own, term)


def mp_sum(term, number):
    ways = lax.axis_size("mp")
    return pl.pallas_call(
        functools.partial(sum_kernel, ways),
        out_shape=jax.ShapeDtypeStruct(term.shape, term.dtype),
        in_specs=in_vmem(1),
        out_specs=pl.BlockSpec(memory_space=pltpu.VMEM),
        scratch_shapes=[pltpu.VMEM((ways - 1,) + term.shape, term.dtype)] + sems(ways),
        compiler_params=params(number),
        cost_estimate=pl.CostEstimate(flops=0, bytes_accessed=term.size * 20, transcendentals=0),
        name="mp_sum",
    )(term)


def column_gather(block, part, plane, parts, number):
    ways = lax.axis_size("mp")
    depth = lax.axis_size("dp") // plane
    rows, width = part.shape[0], part.shape[1] // ways
    up_steps, down_steps = depth // 2, depth - 1 - depth // 2
    sem = pltpu.SemaphoreType.DMA
    return pl.pallas_call(
        functools.partial(column_kernel, ways, plane, parts),
        out_shape=(
            jax.ShapeDtypeStruct((depth,) + block.shape, block.dtype),
            jax.ShapeDtypeStruct((rows, width), jnp.float32),
        ),
        in_specs=in_vmem(2),
        out_specs=tuple(in_vmem(2)),
        scratch_shapes=[pltpu.VMEM((ways - 1, rows, width), part.dtype)]
        + sems(ways)
        + [sem((up_steps * parts,)), sem((up_steps * parts,)), sem((down_steps * parts,)), sem((down_steps * parts,))],
        compiler_params=params(number),
        name="column_gather",
    )(block, part)


def plane_exchange(rows, plane, capacity, number):
    sem = pltpu.SemaphoreType.DMA
    return pl.pallas_call(
        functools.partial(plane_kernel, plane, capacity),
        out_shape=jax.ShapeDtypeStruct(rows.shape, rows.dtype),
        in_specs=in_vmem(1),
        out_specs=pl.BlockSpec(memory_space=pltpu.VMEM),
        scratch_shapes=[sem((plane - 1,)), sem((plane - 1,))],
        compiler_params=params(number),
        name="plane_exchange",
    )(rows)


def encode_part(states, w_in, w_out):
    pre_act = jnp.dot(states, w_in, preferred_element_type=jnp.float32)
    hidden = gelu_value(pre_act).astype(jnp.bfloat16)
    return (pre_act, jnp.dot(hidden, w_out, preferred_element_type=jnp.float32).astype(jnp.bfloat16))


def decode(grad_own, pre_act, out_own, out_full, inv_norm, w_in, w_out, number):
    inv = inv_norm[:, None]
    unit_own = out_own * inv
    dot_part = jnp.sum(unit_own * grad_own, axis=1)
    grad_full, dots = mp_gather_sum(
        grad_own.astype(jnp.bfloat16), jnp.broadcast_to(dot_part[None, :], (8, dot_part.shape[0])), number
    )
    dot_all = dots[0][:, None]
    grad_out = inv * (grad_full.astype(jnp.float32) - out_full.astype(jnp.float32) * (inv * dot_all))
    grad_out_own = inv * (grad_own - unit_own * dot_all)
    contract = (((1,), (1,)), ((), ()))
    grad_hidden = lax.dot_general(
        grad_out.astype(jnp.bfloat16), w_out, contract, preferred_element_type=jnp.float32
    )
    grad_pre = (grad_hidden * gelu_slope(pre_act)).astype(jnp.bfloat16)
    partial_in = lax.dot_general(grad_pre, w_in, contract, preferred_element_type=jnp.float32)
    summed = mp_scatter(partial_in.astype(jnp.bfloat16), number + 1)
    return (summed + grad_out_own).astype(jnp.bfloat16)


def encode(states, w_in, w_out, number):
    pre_act = jnp.dot(states, w_in, preferred_element_type=jnp.float32)
    hidden = gelu_value(pre_act).astype(jnp.bfloat16)
    partial_out = jnp.dot(hidden, w_out, preferred_element_type=jnp.float32).astype(jnp.bfloat16)
    return (pre_act, own_columns(states).astype(jnp.float32) + mp_scatter(partial_out, number))


def shards(query_states, passage_states, w_in, w_out, neg_owner, neg_mask, served_rows, loss_scale):
    owners = lax.axis_size("dp")
    row_count = query_states.shape[0]
    capacity = served_rows.shape[2]
    slots = owners * capacity
    pre_pass, out_pass = encode(passage_states, w_in, w_out, 0)
    half_pass = out_pass.astype(jnp.bfloat16)
    column_width = half_pass.shape[1]

    served = served_rows[0].reshape(-1)
    served_pick = (served[:, None] == jnp.arange(row_count, dtype=jnp.int32)[None, :]).astype(jnp.bfloat16)
    plane, depth = 8, owners // 8
    block = jnp.concatenate(
        [
            half_pass,
            served.astype(jnp.bfloat16).reshape(-1, column_width),
            jnp.zeros((16 - served.shape[0] // column_width, column_width), jnp.bfloat16),
        ],
        axis=0,
    )
    pre_query, part_query = encode_part(query_states, w_in, w_out)
    column, sum_query = column_gather(block, part_query, plane, 3, 7)
    out_query = own_columns(query_states).astype(jnp.float32) + sum_query
    start = (lax.axis_index("dp") // plane) * plane * capacity
    served_here = lax.dynamic_slice(
        column,
        (0, row_count + start // column_width, lax.rem(start, column_width)),
        (depth, 1, plane * capacity),
    ).reshape(depth, plane * capacity)
    wanted = served_here.astype(jnp.int32)[:, :, None] == jnp.arange(row_count, dtype=jnp.int32)[None, None, :]
    chosen = lax.dot_general(
        wanted.astype(jnp.bfloat16),
        column[:, :row_count],
        (((2,), (1,)), ((0,), (0,))),
        preferred_element_type=jnp.float32,
    ).astype(jnp.bfloat16)
    slot_rows = plane_exchange(chosen, plane, capacity, 8).reshape(slots, column_width)
    half_query = out_query.astype(jnp.bfloat16)
    out_full = mp_gather(jnp.concatenate([half_pass, half_query], axis=0), 1)
    owner_rows = neg_owner.T
    named = owner_rows[:, :, None] == jnp.arange(owners, dtype=jnp.int32)[None, None, :]
    names = jnp.any(named, axis=0).astype(jnp.bfloat16)
    spot = jnp.arange(row_count, dtype=jnp.int32)
    earlier = (spot[None, :] < spot[:, None]).astype(jnp.bfloat16)
    before = jnp.dot(earlier, names, preferred_element_type=jnp.float32)
    slot_index = jnp.sum(jnp.where(named, before[None, :, :], 0.0), axis=2).astype(jnp.int32)
    slot_place = owner_rows * capacity + slot_index
    slot_hit = slot_place[:, :, None] == jnp.arange(slots, dtype=jnp.int32)[None, None, :]

    slot_part = lax.dot_general(half_query, slot_rows, (((1,), (1,)), ((), ())), preferred_element_type=jnp.float32)
    slot_wide = slot_rows.astype(jnp.float32)
    slot_square = jnp.sum(slot_wide * slot_wide, axis=1)
    neg_part = jnp.sum(jnp.where(slot_hit, slot_part[None, :, :], 0.0), axis=2)
    neg_square = jnp.sum(jnp.where(slot_hit, slot_square[None, None, :], 0.0), axis=2)
    pos_part = jnp.sum(half_query.astype(jnp.float32) * half_pass.astype(jnp.float32), axis=1)
    squares = jnp.stack([jnp.sum(out_pass * out_pass, axis=1), jnp.sum(out_query * out_query, axis=1)])
    extra = jnp.concatenate([pos_part[None, :], squares, jnp.zeros((5, row_count), jnp.float32)], axis=0)
    sums = mp_sum(jnp.concatenate([neg_part, neg_square, extra], axis=0), 2)
    negatives = neg_owner.shape[1]
    inv_neg = lax.rsqrt(sums[negatives : 2 * negatives] + norm_eps)
    inv_pass = lax.rsqrt(sums[2 * negatives + 1] + norm_eps)
    inv_query = lax.rsqrt(sums[2 * negatives + 2] + norm_eps)
    pos_score = sums[2 * negatives] * inv_query * inv_pass
    neg_score = sums[:negatives] * inv_query[None, :] * inv_neg
    exp_pos = jnp.exp(logit_scale * pos_score)
    exp_neg = neg_mask.T.astype(jnp.float32) * jnp.exp(logit_scale * neg_score)
    denominator = exp_pos + jnp.sum(exp_neg, axis=0)
    factor = loss_scale * logit_scale
    grad_pos = factor * (exp_pos / denominator - 1.0)
    grad_neg = factor * exp_neg / denominator[None, :]

    slot_grad = jnp.sum(jnp.where(slot_hit, (grad_neg * inv_query[None, :])[:, :, None], 0.0), axis=0)
    outgoing_grad = lax.dot_general(
        slot_grad.astype(jnp.bfloat16), half_query, (((0,), (0,)), ((), ())), preferred_element_type=jnp.float32
    ).astype(jnp.bfloat16)
    returned = lax.all_to_all(
        outgoing_grad.reshape(owners, capacity, column_width), "dp", split_axis=0, concat_axis=0, tiled=True
    ).reshape(slots, column_width)
    slot_weight = jnp.sum(jnp.where(slot_hit, (grad_neg * inv_neg)[:, :, None], 0.0), axis=0)
    grad_query_emb = (grad_pos * inv_pass)[:, None] * out_pass + jnp.dot(
        slot_weight.astype(jnp.bfloat16), slot_rows, preferred_element_type=jnp.float32
    )
    grad_query_states = decode(
        grad_query_emb, pre_query, out_query, out_full[row_count:], inv_query, w_in, w_out, 3
    )
    returned, grad_query_states = lax.optimization_barrier((returned, grad_query_states))
    gathered_back = lax.dot_general(
        served_pick, returned, (((0,), (0,)), ((), ())), preferred_element_type=jnp.float32
    )
    grad_pass_emb = (grad_pos * inv_query)[:, None] * out_query + gathered_back
    grad_passage_states = decode(
        grad_pass_emb, pre_pass, out_pass, out_full[:row_count], inv_pass, w_in, w_out, 5
    )
    return (grad_query_states, grad_passage_states)


def solution(mesh):
    in_specs = (
        P("dp", None),
        P("dp", None),
        P(None, "mp"),
        P("mp", None),
        P("dp", None),
        P("dp", None),
        P("dp", None, None),
        P(),
    )
    out_specs = (P("dp", "mp"), P("dp", "mp"))
    return jax.shard_map(shards, mesh=mesh, in_specs=in_specs, out_specs=out_specs, check_vma=False)
```

```python
import functools
import jax
import jax.numpy as jnp
from jax import lax
from jax.experimental import pallas as pl
from jax.experimental.pallas import tpu as pltpu
from jax.sharding import PartitionSpec as P

logit_scale = 50.0
norm_eps = 1e-06
root_half = 0.7071067811865476
inv_root_two_pi = 0.3989422804014327


def gelu_value(values):
    return 0.5 * values * (1.0 + lax.erf(values * root_half))


def gelu_slope(values):
    return (
        0.5 * (1.0 + lax.erf(values * root_half))
        + values * jnp.exp(-0.5 * values * values) * inv_root_two_pi
    )


def own_columns(values):
    column_width = values.shape[1] // lax.axis_size("mp")
    return lax.dynamic_slice_in_dim(values, lax.axis_index("mp") * column_width, column_width, 1)


def greet(ways):
    me = lax.axis_index("mp")
    barrier = pltpu.get_barrier_semaphore()
    for step in range(1, ways):
        pl.semaphore_signal(
            barrier, inc=1, device_id={"mp": lax.rem(me + step, ways)}, device_id_type=pl.DeviceIdType.MESH
        )
    pl.semaphore_wait(barrier, ways - 1)
    return me


def remote(source, target, send_sem, recv_sem, peer):
    return pltpu.make_async_remote_copy(
        src_ref=source,
        dst_ref=target,
        send_sem=send_sem,
        recv_sem=recv_sem,
        device_id={"mp": peer},
        device_id_type=pl.DeviceIdType.MESH,
    )


def block_of(ref, place, width):
    return ref.at[:, pl.ds(pl.multiple_of(place * width, 128), width)]


def scatter_kernel(ways, part_ref, out_ref, landed, send_sem, recv_sem):
    width = out_ref.shape[1]
    me = greet(ways)
    copies = []
    for step in range(1, ways):
        peer = lax.rem(me + step, ways)
        copy = remote(
            block_of(part_ref, peer, width),
            landed.at[step - 1],
            send_sem.at[step - 1],
            recv_sem.at[step - 1],
            peer,
        )
        copy.start()
        copies.append(copy)
    for copy in copies:
        copy.wait()
    own = part_ref[:, pl.ds(pl.multiple_of(me * width, 128), width)]
    total = own.astype(jnp.float32)
    for step in range(1, ways):
        total = total + landed[step - 1].astype(jnp.float32)
    out_ref[...] = total


def gather_kernel(ways, own_ref, out_ref, send_sem, recv_sem):
    width = own_ref.shape[1]
    me = greet(ways)
    copies = []
    for step in range(1, ways):
        copy = remote(
            own_ref,
            block_of(out_ref, me, width),
            send_sem.at[step - 1],
            recv_sem.at[step - 1],
            lax.rem(me + step, ways),
        )
        copy.start()
        copies.append(copy)
    out_ref[:, pl.ds(pl.multiple_of(me * width, 128), width)] = own_ref[...]
    for copy in copies:
        copy.wait()


def gather_sum_kernel(ways, own_ref, term_ref, out_ref, sum_ref, landed, send_sem, recv_sem, term_send, term_recv):
    width = own_ref.shape[1]
    me = greet(ways)
    copies = []
    for step in range(1, ways):
        peer = lax.rem(me + step, ways)
        term_copy = remote(
            term_ref, landed.at[step - 1], term_send.at[step - 1], term_recv.at[step - 1], peer
        )
        copy = remote(
            own_ref, block_of(out_ref, me, width), send_sem.at[step - 1], recv_sem.at[step - 1], peer
        )
        copy.start()
        term_copy.start()
        copies += [copy, term_copy]
    out_ref[:, pl.ds(pl.multiple_of(me * width, 128), width)] = own_ref[...]
    for copy in copies:
        copy.wait()
    total = term_ref[...]
    for step in range(1, ways):
        total = total + landed[step - 1]
    sum_ref[...] = total


def sum_kernel(ways, term_ref, sum_ref, landed, send_sem, recv_sem):
    me = greet(ways)
    copies = []
    for step in range(1, ways):
        copy = remote(
            term_ref,
            landed.at[step - 1],
            send_sem.at[step - 1],
            recv_sem.at[step - 1],
            lax.rem(me + step, ways),
        )
        copy.start()
        copies.append(copy)
    for copy in copies:
        copy.wait()
    total = term_ref[...]
    for step in range(1, ways):
        total = total + landed[step - 1]
    sum_ref[...] = total


def column_kernel(ways, plane, parts, block_ref, part_ref, column_ref, out_ref, landed, mp_send, mp_recv, up_send, up_recv, down_send, down_recv):
    depth, rows = column_ref.shape[0], column_ref.shape[1]
    width = out_ref.shape[1]
    piece = rows // parts
    me, place = lax.axis_index("mp"), lax.axis_index("dp")
    count = depth * plane
    high, here = place // plane, lax.rem(place, plane)
    above = lax.rem(place + plane, count)
    below = lax.rem(place + count - plane, count)
    barrier = pltpu.get_barrier_semaphore()
    for step in range(1, ways):
        pl.semaphore_signal(
            barrier, inc=1, device_id={"mp": lax.rem(me + step, ways)}, device_id_type=pl.DeviceIdType.MESH
        )
    for neighbour in (above, below):
        pl.semaphore_signal(barrier, inc=1, device_id={"dp": neighbour}, device_id_type=pl.DeviceIdType.MESH)
    pl.semaphore_wait(barrier, ways + 1)

    def hop(step, part, upward):
        rank = lax.rem(high + depth - (step - 1), depth) if upward else lax.rem(high + step - 1, depth)
        span = pl.ds(part * piece, piece)
        target = column_ref.at[rank, span]
        return pltpu.make_async_remote_copy(
            src_ref=block_ref.at[span] if step == 1 else target,
            dst_ref=target,
            send_sem=(up_send if upward else down_send).at[(step - 1) * parts + part],
            recv_sem=(up_recv if upward else down_recv).at[(step - 1) * parts + part],
            device_id={"dp": above if upward else below},
            device_id_type=pl.DeviceIdType.MESH,
        )

    up_steps, down_steps = depth // 2, depth - 1 - depth // 2
    hops = {}
    for part in range(parts):
        for upward in (True, False):
            hops[1, part, upward] = hop(1, part, upward)
            hops[1, part, upward].start()
    copies = []
    for step in range(1, ways):
        peer = lax.rem(me + step, ways)
        copy = remote(
            block_of(part_ref, peer, width),
            landed.at[step - 1],
            mp_send.at[step - 1],
            mp_recv.at[step - 1],
            peer,
        )
        copy.start()
        copies.append(copy)
    column_ref[high] = block_ref[...]
    for step in range(2, up_steps + 1):
        for part in range(parts):
            for upward in (True, False):
                hops[step - 1, part, upward].wait_recv() if (step - 1, part, upward) in hops else None
                if upward or step <= down_steps:
                    hops[step, part, upward] = hop(step, part, upward)
                    hops[step, part, upward].start()
    for copy in copies:
        copy.wait()
    own = part_ref[:, pl.ds(pl.multiple_of(me * width, 128), width)]
    total = own.astype(jnp.float32)
    for step in range(1, ways):
        total = total + landed[step - 1].astype(jnp.float32)
    out_ref[...] = total
    for (step, part, upward), copy in hops.items():
        if step == up_steps:
            copy.wait_recv()
        copy.wait_send()


def plane_kernel(plane, capacity, rows_ref, out_ref, send_sem, recv_sem):
    place = lax.axis_index("dp")
    here = lax.rem(place, plane)
    base = place - here
    barrier = pltpu.get_barrier_semaphore()
    for step in range(1, plane):
        pl.semaphore_signal(
            barrier,
            inc=1,
            device_id={"dp": base + lax.rem(here + step, plane)},
            device_id_type=pl.DeviceIdType.MESH,
        )
    pl.semaphore_wait(barrier, plane - 1)
    own = pl.ds(pl.multiple_of(here * capacity, capacity), capacity)
    copies = []
    for step in range(1, plane):
        peer = lax.rem(here + step, plane)
        copy = pltpu.make_async_remote_copy(
            src_ref=rows_ref.at[:, pl.ds(pl.multiple_of(peer * capacity, capacity), capacity)],
            dst_ref=out_ref.at[:, own],
            send_sem=send_sem.at[step - 1],
            recv_sem=recv_sem.at[step - 1],
            device_id={"dp": base + peer},
            device_id_type=pl.DeviceIdType.MESH,
        )
        copy.start()
        copies.append(copy)
    out_ref[:, own] = rows_ref[:, own]
    for copy in copies:
        copy.wait()


def in_vmem(count):
    return [pl.BlockSpec(memory_space=pltpu.VMEM)] * count


def params(number):
    return pltpu.CompilerParams(collective_id=number, has_side_effects=True, vmem_limit_bytes=16 << 20)


def sems(ways):
    return [pltpu.SemaphoreType.DMA((ways - 1,)), pltpu.SemaphoreType.DMA((ways - 1,))]


def mp_scatter(part, number):
    ways = lax.axis_size("mp")
    rows, width = part.shape[0], part.shape[1] // ways
    return pl.pallas_call(
        functools.partial(scatter_kernel, ways),
        out_shape=jax.ShapeDtypeStruct((rows, width), jnp.float32),
        in_specs=in_vmem(1),
        out_specs=pl.BlockSpec(memory_space=pltpu.VMEM),
        scratch_shapes=[pltpu.VMEM((ways - 1, rows, width), part.dtype)] + sems(ways),
        compiler_params=params(number),
        cost_estimate=pl.CostEstimate(flops=rows * width * 4, bytes_accessed=part.size * 4, transcendentals=0),
        name="mp_scatter",
    )(part)


def mp_gather(own, number):
    ways = lax.axis_size("mp")
    rows, width = own.shape
    return pl.pallas_call(
        functools.partial(gather_kernel, ways),
        out_shape=jax.ShapeDtypeStruct((rows, ways * width), own.dtype),
        in_specs=in_vmem(1),
        out_specs=pl.BlockSpec(memory_space=pltpu.VMEM),
        scratch_shapes=sems(ways),
        compiler_params=params(number),
        cost_estimate=pl.CostEstimate(flops=0, bytes_accessed=own.size * 10, transcendentals=0),
        name="mp_gather",
    )(own)


def mp_gather_sum(own, term, number):
    ways = lax.axis_size("mp")
    rows, width = own.shape
    return pl.pallas_call(
        functools.partial(gather_sum_kernel, ways),
        out_shape=(
            jax.ShapeDtypeStruct((rows, ways * width), own.dtype),
            jax.ShapeDtypeStruct(term.shape, term.dtype),
        ),
        in_specs=in_vmem(2),
        out_specs=tuple(in_vmem(2)),
        scratch_shapes=[pltpu.VMEM((ways - 1,) + term.shape, term.dtype)] + sems(ways) + sems(ways),
        compiler_params=params(number),
        cost_estimate=pl.CostEstimate(flops=0, bytes_accessed=own.size * 10, transcendentals=0),
        name="mp_gather_sum",
    )(own, term)


def mp_sum(term, number):
    ways = lax.axis_size("mp")
    return pl.pallas_call(
        functools.partial(sum_kernel, ways),
        out_shape=jax.ShapeDtypeStruct(term.shape, term.dtype),
        in_specs=in_vmem(1),
        out_specs=pl.BlockSpec(memory_space=pltpu.VMEM),
        scratch_shapes=[pltpu.VMEM((ways - 1,) + term.shape, term.dtype)] + sems(ways),
        compiler_params=params(number),
        cost_estimate=pl.CostEstimate(flops=0, bytes_accessed=term.size * 20, transcendentals=0),
        name="mp_sum",
    )(term)


def column_gather(block, part, plane, parts, number):
    ways = lax.axis_size("mp")
    depth = lax.axis_size("dp") // plane
    rows, width = part.shape[0], part.shape[1] // ways
    up_steps, down_steps = depth // 2, depth - 1 - depth // 2
    sem = pltpu.SemaphoreType.DMA
    return pl.pallas_call(
        functools.partial(column_kernel, ways, plane, parts),
        out_shape=(
            jax.ShapeDtypeStruct((depth,) + block.shape, block.dtype),
            jax.ShapeDtypeStruct((rows, width), jnp.float32),
        ),
        in_specs=in_vmem(2),
        out_specs=tuple(in_vmem(2)),
        scratch_shapes=[pltpu.VMEM((ways - 1, rows, width), part.dtype)]
        + sems(ways)
        + [sem((up_steps * parts,)), sem((up_steps * parts,)), sem((down_steps * parts,)), sem((down_steps * parts,))],
        compiler_params=params(number),
        name="column_gather",
    )(block, part)


def plane_exchange(rows, plane, capacity, number):
    sem = pltpu.SemaphoreType.DMA
    return pl.pallas_call(
        functools.partial(plane_kernel, plane, capacity),
        out_shape=jax.ShapeDtypeStruct(rows.shape, rows.dtype),
        in_specs=in_vmem(1),
        out_specs=pl.BlockSpec(memory_space=pltpu.VMEM),
        scratch_shapes=[sem((plane - 1,)), sem((plane - 1,))],
        compiler_params=params(number),
        name="plane_exchange",
    )(rows)


def encode_part(states, w_in, w_out):
    pre_act = jnp.dot(states, w_in, preferred_element_type=jnp.float32)
    hidden = gelu_value(pre_act).astype(jnp.bfloat16)
    return (pre_act, jnp.dot(hidden, w_out, preferred_element_type=jnp.float32).astype(jnp.bfloat16))


def decode(grad_own, pre_act, out_own, out_full, inv_norm, w_in, w_out, number):
    inv = inv_norm[:, None]
    unit_own = out_own * inv
    dot_part = jnp.sum(unit_own * grad_own, axis=1)
    grad_full, dots = mp_gather_sum(
        grad_own.astype(jnp.bfloat16), jnp.broadcast_to(dot_part[None, :], (8, dot_part.shape[0])), number
    )
    dot_all = dots[0][:, None]
    grad_out = inv * (grad_full.astype(jnp.float32) - out_full.astype(jnp.float32) * (inv * dot_all))
    grad_out_own = inv * (grad_own - unit_own * dot_all)
    contract = (((1,), (1,)), ((), ()))
    grad_hidden = lax.dot_general(
        grad_out.astype(jnp.bfloat16), w_out, contract, preferred_element_type=jnp.float32
    )
    grad_pre = (grad_hidden * gelu_slope(pre_act)).astype(jnp.bfloat16)
    partial_in = lax.dot_general(grad_pre, w_in, contract, preferred_element_type=jnp.float32)
    summed = mp_scatter(partial_in.astype(jnp.bfloat16), number + 1)
    return (summed + grad_out_own).astype(jnp.bfloat16)


def encode(states, w_in, w_out, number):
    pre_act = jnp.dot(states, w_in, preferred_element_type=jnp.float32)
    hidden = gelu_value(pre_act).astype(jnp.bfloat16)
    partial_out = jnp.dot(hidden, w_out, preferred_element_type=jnp.float32).astype(jnp.bfloat16)
    return (pre_act, own_columns(states).astype(jnp.float32) + mp_scatter(partial_out, number))


def shards(query_states, passage_states, w_in, w_out, neg_owner, neg_mask, served_rows, loss_scale):
    owners = lax.axis_size("dp")
    row_count = query_states.shape[0]
    capacity = served_rows.shape[2]
    slots = owners * capacity
    pre_pass, out_pass = encode(passage_states, w_in, w_out, 0)
    half_pass = out_pass.astype(jnp.bfloat16)
    column_width = half_pass.shape[1]

    served = served_rows[0].reshape(-1)
    served_pick = (served[:, None] == jnp.arange(row_count, dtype=jnp.int32)[None, :]).astype(jnp.bfloat16)
    plane, depth = 8, owners // 8
    block = jnp.concatenate(
        [
            half_pass,
            served.astype(jnp.bfloat16).reshape(-1, column_width),
            jnp.zeros((16 - served.shape[0] // column_width, column_width), jnp.bfloat16),
        ],
        axis=0,
    )
    pre_query, part_query = encode_part(query_states, w_in, w_out)
    column, sum_query = column_gather(block, part_query, plane, 9, 7)
    out_query = own_columns(query_states).astype(jnp.float32) + sum_query
    start = (lax.axis_index("dp") // plane) * plane * capacity
    served_here = lax.dynamic_slice(
        column,
        (0, row_count + start // column_width, lax.rem(start, column_width)),
        (depth, 1, plane * capacity),
    ).reshape(depth, plane * capacity)
    wanted = served_here.astype(jnp.int32)[:, :, None] == jnp.arange(row_count, dtype=jnp.int32)[None, None, :]
    chosen = lax.dot_general(
        wanted.astype(jnp.bfloat16),
        column[:, :row_count],
        (((2,), (1,)), ((0,), (0,))),
        preferred_element_type=jnp.float32,
    ).astype(jnp.bfloat16)
    slot_rows = plane_exchange(chosen, plane, capacity, 8).reshape(slots, column_width)
    half_query = out_query.astype(jnp.bfloat16)
    out_full = mp_gather(jnp.concatenate([half_pass, half_query], axis=0), 1)
    owner_rows = neg_owner.T
    named = owner_rows[:, :, None] == jnp.arange(owners, dtype=jnp.int32)[None, None, :]
    names = jnp.any(named, axis=0).astype(jnp.bfloat16)
    spot = jnp.arange(row_count, dtype=jnp.int32)
    earlier = (spot[None, :] < spot[:, None]).astype(jnp.bfloat16)
    before = jnp.dot(earlier, names, preferred_element_type=jnp.float32)
    slot_index = jnp.sum(jnp.where(named, before[None, :, :], 0.0), axis=2).astype(jnp.int32)
    slot_place = owner_rows * capacity + slot_index
    slot_hit = slot_place[:, :, None] == jnp.arange(slots, dtype=jnp.int32)[None, None, :]

    slot_part = lax.dot_general(half_query, slot_rows, (((1,), (1,)), ((), ())), preferred_element_type=jnp.float32)
    slot_wide = slot_rows.astype(jnp.float32)
    slot_square = jnp.sum(slot_wide * slot_wide, axis=1)
    neg_part = jnp.sum(jnp.where(slot_hit, slot_part[None, :, :], 0.0), axis=2)
    neg_square = jnp.sum(jnp.where(slot_hit, slot_square[None, None, :], 0.0), axis=2)
    pos_part = jnp.sum(half_query.astype(jnp.float32) * half_pass.astype(jnp.float32), axis=1)
    squares = jnp.stack([jnp.sum(out_pass * out_pass, axis=1), jnp.sum(out_query * out_query, axis=1)])
    extra = jnp.concatenate([pos_part[None, :], squares, jnp.zeros((5, row_count), jnp.float32)], axis=0)
    sums = mp_sum(jnp.concatenate([neg_part, neg_square, extra], axis=0), 2)
    negatives = neg_owner.shape[1]
    inv_neg = lax.rsqrt(sums[negatives : 2 * negatives] + norm_eps)
    inv_pass = lax.rsqrt(sums[2 * negatives + 1] + norm_eps)
    inv_query = lax.rsqrt(sums[2 * negatives + 2] + norm_eps)
    pos_score = sums[2 * negatives] * inv_query * inv_pass
    neg_score = sums[:negatives] * inv_query[None, :] * inv_neg
    exp_pos = jnp.exp(logit_scale * pos_score)
    exp_neg = neg_mask.T.astype(jnp.float32) * jnp.exp(logit_scale * neg_score)
    denominator = exp_pos + jnp.sum(exp_neg, axis=0)
    factor = loss_scale * logit_scale
    grad_pos = factor * (exp_pos / denominator - 1.0)
    grad_neg = factor * exp_neg / denominator[None, :]

    slot_grad = jnp.sum(jnp.where(slot_hit, (grad_neg * inv_query[None, :])[:, :, None], 0.0), axis=0)
    outgoing_grad = lax.dot_general(
        slot_grad.astype(jnp.bfloat16), half_query, (((0,), (0,)), ((), ())), preferred_element_type=jnp.float32
    ).astype(jnp.bfloat16)
    late_weight, outgoing_grad = lax.optimization_barrier((grad_neg * inv_neg, outgoing_grad))
    returned = lax.all_to_all(
        outgoing_grad.reshape(owners, capacity, column_width), "dp", split_axis=0, concat_axis=0, tiled=True
    ).reshape(slots, column_width)
    slot_weight = jnp.sum(jnp.where(slot_hit, late_weight[:, :, None], 0.0), axis=0)
    grad_query_emb = (grad_pos * inv_pass)[:, None] * out_pass + jnp.dot(
        slot_weight.astype(jnp.bfloat16), slot_rows, preferred_element_type=jnp.float32
    )
    grad_query_states = decode(
        grad_query_emb, pre_query, out_query, out_full[row_count:], inv_query, w_in, w_out, 3
    )
    returned, grad_query_states = lax.optimization_barrier((returned, grad_query_states))
    gathered_back = lax.dot_general(
        served_pick, returned, (((0,), (0,)), ((), ())), preferred_element_type=jnp.float32
    )
    grad_pass_emb = (grad_pos * inv_query)[:, None] * out_query + gathered_back
    grad_passage_states = decode(
        grad_pass_emb, pre_pass, out_pass, out_full[:row_count], inv_pass, w_in, w_out, 5
    )
    return (grad_query_states, grad_passage_states)


def solution(mesh):
    in_specs = (
        P("dp", None),
        P("dp", None),
        P(None, "mp"),
        P("mp", None),
        P("dp", None),
        P("dp", None),
        P("dp", None, None),
        P(),
    )
    out_specs = (P("dp", "mp"), P("dp", "mp"))
    return jax.shard_map(shards, mesh=mesh, in_specs=in_specs, out_specs=out_specs, check_vma=False)
```

```python
import functools
import jax
import jax.numpy as jnp
from jax import lax
from jax.experimental import pallas as pl
from jax.experimental.pallas import tpu as pltpu
from jax.sharding import PartitionSpec as P

logit_scale = 50.0
norm_eps = 1e-06
root_half = 0.7071067811865476
inv_root_two_pi = 0.3989422804014327


def gelu_value(values):
    return 0.5 * values * (1.0 + lax.erf(values * root_half))


def gelu_slope(values):
    return (
        0.5 * (1.0 + lax.erf(values * root_half))
        + values * jnp.exp(-0.5 * values * values) * inv_root_two_pi
    )


def own_columns(values):
    column_width = values.shape[1] // lax.axis_size("mp")
    return lax.dynamic_slice_in_dim(values, lax.axis_index("mp") * column_width, column_width, 1)


def greet(ways):
    me = lax.axis_index("mp")
    barrier = pltpu.get_barrier_semaphore()
    for step in range(1, ways):
        pl.semaphore_signal(
            barrier, inc=1, device_id={"mp": lax.rem(me + step, ways)}, device_id_type=pl.DeviceIdType.MESH
        )
    pl.semaphore_wait(barrier, ways - 1)
    return me


def remote(source, target, send_sem, recv_sem, peer):
    return pltpu.make_async_remote_copy(
        src_ref=source,
        dst_ref=target,
        send_sem=send_sem,
        recv_sem=recv_sem,
        device_id={"mp": peer},
        device_id_type=pl.DeviceIdType.MESH,
    )


def block_of(ref, place, width):
    return ref.at[:, pl.ds(pl.multiple_of(place * width, 128), width)]


def scatter_kernel(ways, part_ref, out_ref, landed, send_sem, recv_sem):
    width = out_ref.shape[1]
    me = greet(ways)
    copies = []
    for step in range(1, ways):
        peer = lax.rem(me + step, ways)
        copy = remote(
            block_of(part_ref, peer, width),
            landed.at[step - 1],
            send_sem.at[step - 1],
            recv_sem.at[step - 1],
            peer,
        )
        copy.start()
        copies.append(copy)
    for copy in copies:
        copy.wait()
    own = part_ref[:, pl.ds(pl.multiple_of(me * width, 128), width)]
    total = own.astype(jnp.float32)
    for step in range(1, ways):
        total = total + landed[step - 1].astype(jnp.float32)
    out_ref[...] = total


def gather_kernel(ways, own_ref, out_ref, send_sem, recv_sem):
    width = own_ref.shape[1]
    me = greet(ways)
    copies = []
    for step in range(1, ways):
        copy = remote(
            own_ref,
            block_of(out_ref, me, width),
            send_sem.at[step - 1],
            recv_sem.at[step - 1],
            lax.rem(me + step, ways),
        )
        copy.start()
        copies.append(copy)
    out_ref[:, pl.ds(pl.multiple_of(me * width, 128), width)] = own_ref[...]
    for copy in copies:
        copy.wait()


def gather_sum_kernel(ways, own_ref, term_ref, out_ref, sum_ref, landed, send_sem, recv_sem, term_send, term_recv):
    width = own_ref.shape[1]
    me = greet(ways)
    copies = []
    for step in range(1, ways):
        peer = lax.rem(me + step, ways)
        term_copy = remote(
            term_ref, landed.at[step - 1], term_send.at[step - 1], term_recv.at[step - 1], peer
        )
        copy = remote(
            own_ref, block_of(out_ref, me, width), send_sem.at[step - 1], recv_sem.at[step - 1], peer
        )
        copy.start()
        term_copy.start()
        copies += [copy, term_copy]
    out_ref[:, pl.ds(pl.multiple_of(me * width, 128), width)] = own_ref[...]
    for copy in copies:
        copy.wait()
    total = term_ref[...]
    for step in range(1, ways):
        total = total + landed[step - 1]
    sum_ref[...] = total


def sum_kernel(ways, term_ref, sum_ref, landed, send_sem, recv_sem):
    me = greet(ways)
    copies = []
    for step in range(1, ways):
        copy = remote(
            term_ref,
            landed.at[step - 1],
            send_sem.at[step - 1],
            recv_sem.at[step - 1],
            lax.rem(me + step, ways),
        )
        copy.start()
        copies.append(copy)
    for copy in copies:
        copy.wait()
    total = term_ref[...]
    for step in range(1, ways):
        total = total + landed[step - 1]
    sum_ref[...] = total


def column_kernel(ways, plane, parts, block_ref, part_ref, column_ref, out_ref, landed, mp_send, mp_recv, up_send, up_recv, down_send, down_recv):
    depth, rows = column_ref.shape[0], column_ref.shape[1]
    width = out_ref.shape[1]
    piece = rows // parts
    me, place = lax.axis_index("mp"), lax.axis_index("dp")
    count = depth * plane
    high, here = place // plane, lax.rem(place, plane)
    above = lax.rem(place + plane, count)
    below = lax.rem(place + count - plane, count)
    barrier = pltpu.get_barrier_semaphore()
    for step in range(1, ways):
        pl.semaphore_signal(
            barrier, inc=1, device_id={"mp": lax.rem(me + step, ways)}, device_id_type=pl.DeviceIdType.MESH
        )
    for neighbour in (above, below):
        pl.semaphore_signal(barrier, inc=1, device_id={"dp": neighbour}, device_id_type=pl.DeviceIdType.MESH)
    pl.semaphore_wait(barrier, ways + 1)

    def hop(step, part, upward):
        rank = lax.rem(high + depth - (step - 1), depth) if upward else lax.rem(high + step - 1, depth)
        span = pl.ds(part * piece, piece)
        target = column_ref.at[rank, span]
        return pltpu.make_async_remote_copy(
            src_ref=block_ref.at[span] if step == 1 else target,
            dst_ref=target,
            send_sem=(up_send if upward else down_send).at[(step - 1) * parts + part],
            recv_sem=(up_recv if upward else down_recv).at[(step - 1) * parts + part],
            device_id={"dp": above if upward else below},
            device_id_type=pl.DeviceIdType.MESH,
        )

    up_steps, down_steps = depth // 2, depth - 1 - depth // 2
    hops = {}
    for part in range(parts):
        for upward in (True, False):
            hops[1, part, upward] = hop(1, part, upward)
            hops[1, part, upward].start()
    copies = []
    for step in range(1, ways):
        peer = lax.rem(me + step, ways)
        copy = remote(
            block_of(part_ref, peer, width),
            landed.at[step - 1],
            mp_send.at[step - 1],
            mp_recv.at[step - 1],
            peer,
        )
        copy.start()
        copies.append(copy)
    column_ref[high] = block_ref[...]
    for step in range(2, up_steps + 1):
        for part in range(parts):
            for upward in (True, False):
                hops[step - 1, part, upward].wait_recv() if (step - 1, part, upward) in hops else None
                if upward or step <= down_steps:
                    hops[step, part, upward] = hop(step, part, upward)
                    hops[step, part, upward].start()
    for copy in copies:
        copy.wait()
    own = part_ref[:, pl.ds(pl.multiple_of(me * width, 128), width)]
    total = own.astype(jnp.float32)
    for step in range(1, ways):
        total = total + landed[step - 1].astype(jnp.float32)
    out_ref[...] = total
    for (step, part, upward), copy in hops.items():
        if step == up_steps:
            copy.wait_recv()
        copy.wait_send()


def plane_kernel(plane, capacity, rows_ref, out_ref, held, send_sem, recv_sem, out_send, out_recv, on_send, on_recv):
    place = lax.axis_index("dp")
    here = lax.rem(place, plane)
    base = place - here
    chips, half = plane // 2, rows_ref.shape[0] // 2
    chip, core = here // 2, lax.rem(here, 2)

    def at(chip_step, core_index):
        return lax.rem(chip + chip_step, chips) * 2 + core_index

    def span(index):
        return pl.ds(pl.multiple_of(index * capacity, capacity), capacity)

    def copy_to(source, target, send, recv, peer):
        return pltpu.make_async_remote_copy(
            src_ref=source,
            dst_ref=target,
            send_sem=send,
            recv_sem=recv,
            device_id={"dp": base + peer},
            device_id_type=pl.DeviceIdType.MESH,
        )

    near = [at(1, core), at(1, 1 - core), at(chips - 1, core), at(chips - 1, 1 - core), at(0, 1 - core)]
    barrier = pltpu.get_barrier_semaphore()
    for peer in near:
        pl.semaphore_signal(barrier, inc=1, device_id={"dp": base + peer}, device_id_type=pl.DeviceIdType.MESH)
    pl.semaphore_wait(barrier, len(near))
    ways = (1, chips - 1)
    first = []
    for which, way in enumerate(ways):
        for target_core in range(2):
            slot = which * 2 + target_core
            copy = copy_to(
                rows_ref.at[pl.ds(which * half, half), span(at(2, target_core))],
                held.at[slot],
                out_send.at[slot],
                out_recv.at[slot],
                at(way, core),
            )
            copy.start()
            first.append(copy)
    copies = []
    for step, peer in enumerate(near):
        copy = copy_to(
            rows_ref.at[:, span(peer)], out_ref.at[:, span(here)], send_sem.at[step], recv_sem.at[step], peer
        )
        copy.start()
        copies.append(copy)
    out_ref[:, span(here)] = rows_ref[:, span(here)]
    second = []
    for which, way in enumerate(ways):
        for target_core in range(2):
            slot = which * 2 + target_core
            first[slot].wait_recv()
            copy = copy_to(
                held.at[slot],
                out_ref.at[pl.ds(which * half, half), span(at(chips - way, core))],
                on_send.at[slot],
                on_recv.at[which * 2 + core],
                at(way, target_core),
            )
            copy.start()
            second.append(copy)
    for copy in copies:
        copy.wait()
    for which, way in enumerate(ways):
        for source_core in range(2):
            slot = which * 2 + source_core
            copy_to(
                held.at[slot],
                out_ref.at[pl.ds(which * half, half), span(at(2, source_core))],
                on_send.at[slot],
                on_recv.at[slot],
                at(way, source_core),
            ).wait_recv()
    for copy in first + second:
        copy.wait_send()


def in_vmem(count):
    return [pl.BlockSpec(memory_space=pltpu.VMEM)] * count


def params(number):
    return pltpu.CompilerParams(collective_id=number, has_side_effects=True, vmem_limit_bytes=16 << 20)


def sems(ways):
    return [pltpu.SemaphoreType.DMA((ways - 1,)), pltpu.SemaphoreType.DMA((ways - 1,))]


def mp_scatter(part, number):
    ways = lax.axis_size("mp")
    rows, width = part.shape[0], part.shape[1] // ways
    return pl.pallas_call(
        functools.partial(scatter_kernel, ways),
        out_shape=jax.ShapeDtypeStruct((rows, width), jnp.float32),
        in_specs=in_vmem(1),
        out_specs=pl.BlockSpec(memory_space=pltpu.VMEM),
        scratch_shapes=[pltpu.VMEM((ways - 1, rows, width), part.dtype)] + sems(ways),
        compiler_params=params(number),
        cost_estimate=pl.CostEstimate(flops=rows * width * 4, bytes_accessed=part.size * 4, transcendentals=0),
        name="mp_scatter",
    )(part)


def mp_gather(own, number):
    ways = lax.axis_size("mp")
    rows, width = own.shape
    return pl.pallas_call(
        functools.partial(gather_kernel, ways),
        out_shape=jax.ShapeDtypeStruct((rows, ways * width), own.dtype),
        in_specs=in_vmem(1),
        out_specs=pl.BlockSpec(memory_space=pltpu.VMEM),
        scratch_shapes=sems(ways),
        compiler_params=params(number),
        cost_estimate=pl.CostEstimate(flops=0, bytes_accessed=own.size * 10, transcendentals=0),
        name="mp_gather",
    )(own)


def mp_gather_sum(own, term, number):
    ways = lax.axis_size("mp")
    rows, width = own.shape
    return pl.pallas_call(
        functools.partial(gather_sum_kernel, ways),
        out_shape=(
            jax.ShapeDtypeStruct((rows, ways * width), own.dtype),
            jax.ShapeDtypeStruct(term.shape, term.dtype),
        ),
        in_specs=in_vmem(2),
        out_specs=tuple(in_vmem(2)),
        scratch_shapes=[pltpu.VMEM((ways - 1,) + term.shape, term.dtype)] + sems(ways) + sems(ways),
        compiler_params=params(number),
        cost_estimate=pl.CostEstimate(flops=0, bytes_accessed=own.size * 10, transcendentals=0),
        name="mp_gather_sum",
    )(own, term)


def mp_sum(term, number):
    ways = lax.axis_size("mp")
    return pl.pallas_call(
        functools.partial(sum_kernel, ways),
        out_shape=jax.ShapeDtypeStruct(term.shape, term.dtype),
        in_specs=in_vmem(1),
        out_specs=pl.BlockSpec(memory_space=pltpu.VMEM),
        scratch_shapes=[pltpu.VMEM((ways - 1,) + term.shape, term.dtype)] + sems(ways),
        compiler_params=params(number),
        cost_estimate=pl.CostEstimate(flops=0, bytes_accessed=term.size * 20, transcendentals=0),
        name="mp_sum",
    )(term)


def column_gather(block, part, plane, parts, number):
    ways = lax.axis_size("mp")
    depth = lax.axis_size("dp") // plane
    rows, width = part.shape[0], part.shape[1] // ways
    up_steps, down_steps = depth // 2, depth - 1 - depth // 2
    sem = pltpu.SemaphoreType.DMA
    return pl.pallas_call(
        functools.partial(column_kernel, ways, plane, parts),
        out_shape=(
            jax.ShapeDtypeStruct((depth,) + block.shape, block.dtype),
            jax.ShapeDtypeStruct((rows, width), jnp.float32),
        ),
        in_specs=in_vmem(2),
        out_specs=tuple(in_vmem(2)),
        scratch_shapes=[pltpu.VMEM((ways - 1, rows, width), part.dtype)]
        + sems(ways)
        + [sem((up_steps * parts,)), sem((up_steps * parts,)), sem((down_steps * parts,)), sem((down_steps * parts,))],
        compiler_params=params(number),
        name="column_gather",
    )(block, part)


def plane_exchange(rows, plane, capacity, number):
    sem = pltpu.SemaphoreType.DMA
    return pl.pallas_call(
        functools.partial(plane_kernel, plane, capacity),
        out_shape=jax.ShapeDtypeStruct(rows.shape, rows.dtype),
        in_specs=in_vmem(1),
        out_specs=pl.BlockSpec(memory_space=pltpu.VMEM),
        scratch_shapes=[pltpu.VMEM((4, rows.shape[0] // 2, capacity, rows.shape[2]), rows.dtype)]
        + [sem((5,)), sem((5,)), sem((4,)), sem((4,)), sem((4,)), sem((4,))],
        compiler_params=params(number),
        name="plane_exchange",
    )(rows)


def encode_part(states, w_in, w_out):
    pre_act = jnp.dot(states, w_in, preferred_element_type=jnp.float32)
    hidden = gelu_value(pre_act).astype(jnp.bfloat16)
    return (pre_act, jnp.dot(hidden, w_out, preferred_element_type=jnp.float32).astype(jnp.bfloat16))


def decode(grad_own, pre_act, out_own, out_full, inv_norm, w_in, w_out, number):
    inv = inv_norm[:, None]
    unit_own = out_own * inv
    dot_part = jnp.sum(unit_own * grad_own, axis=1)
    grad_full, dots = mp_gather_sum(
        grad_own.astype(jnp.bfloat16), jnp.broadcast_to(dot_part[None, :], (8, dot_part.shape[0])), number
    )
    dot_all = dots[0][:, None]
    grad_out = inv * (grad_full.astype(jnp.float32) - out_full.astype(jnp.float32) * (inv * dot_all))
    grad_out_own = inv * (grad_own - unit_own * dot_all)
    contract = (((1,), (1,)), ((), ()))
    grad_hidden = lax.dot_general(
        grad_out.astype(jnp.bfloat16), w_out, contract, preferred_element_type=jnp.float32
    )
    grad_pre = (grad_hidden * gelu_slope(pre_act)).astype(jnp.bfloat16)
    partial_in = lax.dot_general(grad_pre, w_in, contract, preferred_element_type=jnp.float32)
    summed = mp_scatter(partial_in.astype(jnp.bfloat16), number + 1)
    return (summed + grad_out_own).astype(jnp.bfloat16)


def encode(states, w_in, w_out, number):
    pre_act = jnp.dot(states, w_in, preferred_element_type=jnp.float32)
    hidden = gelu_value(pre_act).astype(jnp.bfloat16)
    partial_out = jnp.dot(hidden, w_out, preferred_element_type=jnp.float32).astype(jnp.bfloat16)
    return (pre_act, own_columns(states).astype(jnp.float32) + mp_scatter(partial_out, number))


def shards(query_states, passage_states, w_in, w_out, neg_owner, neg_mask, served_rows, loss_scale):
    owners = lax.axis_size("dp")
    row_count = query_states.shape[0]
    capacity = served_rows.shape[2]
    slots = owners * capacity
    pre_pass, out_pass = encode(passage_states, w_in, w_out, 0)
    half_pass = out_pass.astype(jnp.bfloat16)
    column_width = half_pass.shape[1]

    served = served_rows[0].reshape(-1)
    served_pick = (served[:, None] == jnp.arange(row_count, dtype=jnp.int32)[None, :]).astype(jnp.bfloat16)
    plane, depth = 8, owners // 8
    block = jnp.concatenate(
        [
            half_pass,
            served.astype(jnp.bfloat16).reshape(-1, column_width),
            jnp.zeros((16 - served.shape[0] // column_width, column_width), jnp.bfloat16),
        ],
        axis=0,
    )
    pre_query, part_query = encode_part(query_states, w_in, w_out)
    column, sum_query = column_gather(block, part_query, plane, 3, 7)
    out_query = own_columns(query_states).astype(jnp.float32) + sum_query
    start = (lax.axis_index("dp") // plane) * plane * capacity
    served_here = lax.dynamic_slice(
        column,
        (0, row_count + start // column_width, lax.rem(start, column_width)),
        (depth, 1, plane * capacity),
    ).reshape(depth, plane * capacity)
    wanted = served_here.astype(jnp.int32)[:, :, None] == jnp.arange(row_count, dtype=jnp.int32)[None, None, :]
    chosen = lax.dot_general(
        wanted.astype(jnp.bfloat16),
        column[:, :row_count],
        (((2,), (1,)), ((0,), (0,))),
        preferred_element_type=jnp.float32,
    ).astype(jnp.bfloat16)
    slot_rows = plane_exchange(chosen, plane, capacity, 8).reshape(slots, column_width)
    half_query = out_query.astype(jnp.bfloat16)
    out_full = mp_gather(jnp.concatenate([half_pass, half_query], axis=0), 1)
    owner_rows = neg_owner.T
    named = owner_rows[:, :, None] == jnp.arange(owners, dtype=jnp.int32)[None, None, :]
    names = jnp.any(named, axis=0).astype(jnp.bfloat16)
    spot = jnp.arange(row_count, dtype=jnp.int32)
    earlier = (spot[None, :] < spot[:, None]).astype(jnp.bfloat16)
    before = jnp.dot(earlier, names, preferred_element_type=jnp.float32)
    slot_index = jnp.sum(jnp.where(named, before[None, :, :], 0.0), axis=2).astype(jnp.int32)
    slot_place = owner_rows * capacity + slot_index
    slot_hit = slot_place[:, :, None] == jnp.arange(slots, dtype=jnp.int32)[None, None, :]

    slot_part = lax.dot_general(half_query, slot_rows, (((1,), (1,)), ((), ())), preferred_element_type=jnp.float32)
    slot_wide = slot_rows.astype(jnp.float32)
    slot_square = jnp.sum(slot_wide * slot_wide, axis=1)
    neg_part = jnp.sum(jnp.where(slot_hit, slot_part[None, :, :], 0.0), axis=2)
    neg_square = jnp.sum(jnp.where(slot_hit, slot_square[None, None, :], 0.0), axis=2)
    pos_part = jnp.sum(half_query.astype(jnp.float32) * half_pass.astype(jnp.float32), axis=1)
    squares = jnp.stack([jnp.sum(out_pass * out_pass, axis=1), jnp.sum(out_query * out_query, axis=1)])
    extra = jnp.concatenate([pos_part[None, :], squares, jnp.zeros((5, row_count), jnp.float32)], axis=0)
    sums = mp_sum(jnp.concatenate([neg_part, neg_square, extra], axis=0), 2)
    negatives = neg_owner.shape[1]
    inv_neg = lax.rsqrt(sums[negatives : 2 * negatives] + norm_eps)
    inv_pass = lax.rsqrt(sums[2 * negatives + 1] + norm_eps)
    inv_query = lax.rsqrt(sums[2 * negatives + 2] + norm_eps)
    pos_score = sums[2 * negatives] * inv_query * inv_pass
    neg_score = sums[:negatives] * inv_query[None, :] * inv_neg
    exp_pos = jnp.exp(logit_scale * pos_score)
    exp_neg = neg_mask.T.astype(jnp.float32) * jnp.exp(logit_scale * neg_score)
    denominator = exp_pos + jnp.sum(exp_neg, axis=0)
    factor = loss_scale * logit_scale
    grad_pos = factor * (exp_pos / denominator - 1.0)
    grad_neg = factor * exp_neg / denominator[None, :]

    slot_grad = jnp.sum(jnp.where(slot_hit, (grad_neg * inv_query[None, :])[:, :, None], 0.0), axis=0)
    outgoing_grad = lax.dot_general(
        slot_grad.astype(jnp.bfloat16), half_query, (((0,), (0,)), ((), ())), preferred_element_type=jnp.float32
    ).astype(jnp.bfloat16)
    returned = lax.all_to_all(
        outgoing_grad.reshape(owners, capacity, column_width), "dp", split_axis=0, concat_axis=0, tiled=True
    ).reshape(slots, column_width)
    slot_weight = jnp.sum(jnp.where(slot_hit, (grad_neg * inv_neg)[:, :, None], 0.0), axis=0)
    grad_query_emb = (grad_pos * inv_pass)[:, None] * out_pass + jnp.dot(
        slot_weight.astype(jnp.bfloat16), slot_rows, preferred_element_type=jnp.float32
    )
    grad_query_states = decode(
        grad_query_emb, pre_query, out_query, out_full[row_count:], inv_query, w_in, w_out, 3
    )
    returned, grad_query_states = lax.optimization_barrier((returned, grad_query_states))
    gathered_back = lax.dot_general(
        served_pick, returned, (((0,), (0,)), ((), ())), preferred_element_type=jnp.float32
    )
    grad_pass_emb = (grad_pos * inv_query)[:, None] * out_query + gathered_back
    grad_passage_states = decode(
        grad_pass_emb, pre_pass, out_pass, out_full[:row_count], inv_pass, w_in, w_out, 5
    )
    return (grad_query_states, grad_passage_states)


def solution(mesh):
    in_specs = (
        P("dp", None),
        P("dp", None),
        P(None, "mp"),
        P("mp", None),
        P("dp", None),
        P("dp", None),
        P("dp", None, None),
        P(),
    )
    out_specs = (P("dp", "mp"), P("dp", "mp"))
    return jax.shard_map(shards, mesh=mesh, in_specs=in_specs, out_specs=out_specs, check_vma=False)
```

```python
import functools
import jax
import jax.numpy as jnp
from jax import lax
from jax.experimental import pallas as pl
from jax.experimental.pallas import tpu as pltpu
from jax.sharding import PartitionSpec as P

logit_scale = 50.0
norm_eps = 1e-06
root_half = 0.7071067811865476
inv_root_two_pi = 0.3989422804014327


def gelu_value(values):
    return 0.5 * values * (1.0 + lax.erf(values * root_half))


def gelu_slope(values):
    return (
        0.5 * (1.0 + lax.erf(values * root_half))
        + values * jnp.exp(-0.5 * values * values) * inv_root_two_pi
    )


def own_columns(values):
    column_width = values.shape[1] // lax.axis_size("mp")
    return lax.dynamic_slice_in_dim(values, lax.axis_index("mp") * column_width, column_width, 1)


def greet(ways):
    me = lax.axis_index("mp")
    barrier = pltpu.get_barrier_semaphore()
    for step in range(1, ways):
        pl.semaphore_signal(
            barrier, inc=1, device_id={"mp": lax.rem(me + step, ways)}, device_id_type=pl.DeviceIdType.MESH
        )
    pl.semaphore_wait(barrier, ways - 1)
    return me


def remote(source, target, send_sem, recv_sem, peer):
    return pltpu.make_async_remote_copy(
        src_ref=source,
        dst_ref=target,
        send_sem=send_sem,
        recv_sem=recv_sem,
        device_id={"mp": peer},
        device_id_type=pl.DeviceIdType.MESH,
    )


def block_of(ref, place, width):
    return ref.at[:, pl.ds(pl.multiple_of(place * width, 128), width)]


def scatter_kernel(ways, part_ref, out_ref, landed, send_sem, recv_sem):
    width = out_ref.shape[1]
    me = greet(ways)
    copies = []
    for step in range(1, ways):
        peer = lax.rem(me + step, ways)
        copy = remote(
            block_of(part_ref, peer, width),
            landed.at[step - 1],
            send_sem.at[step - 1],
            recv_sem.at[step - 1],
            peer,
        )
        copy.start()
        copies.append(copy)
    for copy in copies:
        copy.wait()
    own = part_ref[:, pl.ds(pl.multiple_of(me * width, 128), width)]
    total = own.astype(jnp.float32)
    for step in range(1, ways):
        total = total + landed[step - 1].astype(jnp.float32)
    out_ref[...] = total


def gather_kernel(ways, own_ref, out_ref, send_sem, recv_sem):
    width = own_ref.shape[1]
    me = greet(ways)
    copies = []
    for step in range(1, ways):
        copy = remote(
            own_ref,
            block_of(out_ref, me, width),
            send_sem.at[step - 1],
            recv_sem.at[step - 1],
            lax.rem(me + step, ways),
        )
        copy.start()
        copies.append(copy)
    out_ref[:, pl.ds(pl.multiple_of(me * width, 128), width)] = own_ref[...]
    for copy in copies:
        copy.wait()


def gather_sum_kernel(ways, own_ref, term_ref, out_ref, sum_ref, landed, send_sem, recv_sem, term_send, term_recv):
    width = own_ref.shape[1]
    me = greet(ways)
    copies = []
    for step in range(1, ways):
        peer = lax.rem(me + step, ways)
        term_copy = remote(
            term_ref, landed.at[step - 1], term_send.at[step - 1], term_recv.at[step - 1], peer
        )
        copy = remote(
            own_ref, block_of(out_ref, me, width), send_sem.at[step - 1], recv_sem.at[step - 1], peer
        )
        copy.start()
        term_copy.start()
        copies += [copy, term_copy]
    out_ref[:, pl.ds(pl.multiple_of(me * width, 128), width)] = own_ref[...]
    for copy in copies:
        copy.wait()
    total = term_ref[...]
    for step in range(1, ways):
        total = total + landed[step - 1]
    sum_ref[...] = total


def sum_kernel(ways, term_ref, sum_ref, landed, send_sem, recv_sem):
    me = greet(ways)
    copies = []
    for step in range(1, ways):
        copy = remote(
            term_ref,
            landed.at[step - 1],
            send_sem.at[step - 1],
            recv_sem.at[step - 1],
            lax.rem(me + step, ways),
        )
        copy.start()
        copies.append(copy)
    for copy in copies:
        copy.wait()
    total = term_ref[...]
    for step in range(1, ways):
        total = total + landed[step - 1]
    sum_ref[...] = total


def column_kernel(ways, plane, parts, block_ref, part_ref, column_ref, out_ref, landed, mp_send, mp_recv, up_send, up_recv, down_send, down_recv):
    depth, rows = column_ref.shape[0], column_ref.shape[1]
    width = out_ref.shape[1]
    piece = rows // parts
    me, place = lax.axis_index("mp"), lax.axis_index("dp")
    count = depth * plane
    high, here = place // plane, lax.rem(place, plane)
    above = lax.rem(place + plane, count)
    below = lax.rem(place + count - plane, count)
    barrier = pltpu.get_barrier_semaphore()
    for step in range(1, ways):
        pl.semaphore_signal(
            barrier, inc=1, device_id={"mp": lax.rem(me + step, ways)}, device_id_type=pl.DeviceIdType.MESH
        )
    for neighbour in (above, below):
        pl.semaphore_signal(barrier, inc=1, device_id={"dp": neighbour}, device_id_type=pl.DeviceIdType.MESH)
    pl.semaphore_wait(barrier, ways + 1)

    def hop(step, part, upward):
        rank = lax.rem(high + depth - (step - 1), depth) if upward else lax.rem(high + step - 1, depth)
        span = pl.ds(part * piece, piece)
        target = column_ref.at[rank, span]
        return pltpu.make_async_remote_copy(
            src_ref=block_ref.at[span] if step == 1 else target,
            dst_ref=target,
            send_sem=(up_send if upward else down_send).at[(step - 1) * parts + part],
            recv_sem=(up_recv if upward else down_recv).at[(step - 1) * parts + part],
            device_id={"dp": above if upward else below},
            device_id_type=pl.DeviceIdType.MESH,
        )

    up_steps, down_steps = depth // 2, depth - 1 - depth // 2
    hops = {}
    for part in range(parts):
        for upward in (True, False):
            hops[1, part, upward] = hop(1, part, upward)
            hops[1, part, upward].start()
    copies = []
    for step in range(1, ways):
        peer = lax.rem(me + step, ways)
        copy = remote(
            block_of(part_ref, peer, width),
            landed.at[step - 1],
            mp_send.at[step - 1],
            mp_recv.at[step - 1],
            peer,
        )
        copy.start()
        copies.append(copy)
    column_ref[high] = block_ref[...]
    for step in range(2, up_steps + 1):
        for part in range(parts):
            for upward in (True, False):
                hops[step - 1, part, upward].wait_recv() if (step - 1, part, upward) in hops else None
                if upward or step <= down_steps:
                    hops[step, part, upward] = hop(step, part, upward)
                    hops[step, part, upward].start()
    for copy in copies:
        copy.wait()
    own = part_ref[:, pl.ds(pl.multiple_of(me * width, 128), width)]
    total = own.astype(jnp.float32)
    for step in range(1, ways):
        total = total + landed[step - 1].astype(jnp.float32)
    out_ref[...] = total
    for (step, part, upward), copy in hops.items():
        if step == up_steps:
            copy.wait_recv()
        copy.wait_send()


def plane_kernel(plane, capacity, rows_ref, out_ref, send_sem, recv_sem):
    place = lax.axis_index("dp")
    here = lax.rem(place, plane)
    base = place - here
    barrier = pltpu.get_barrier_semaphore()
    for step in range(1, plane):
        pl.semaphore_signal(
            barrier,
            inc=1,
            device_id={"dp": base + lax.rem(here + step, plane)},
            device_id_type=pl.DeviceIdType.MESH,
        )
    pl.semaphore_wait(barrier, plane - 1)
    own = pl.ds(pl.multiple_of(here * capacity, capacity), capacity)
    copies = []
    for step in range(1, plane):
        peer = lax.rem(here + step, plane)
        copy = pltpu.make_async_remote_copy(
            src_ref=rows_ref.at[:, pl.ds(pl.multiple_of(peer * capacity, capacity), capacity)],
            dst_ref=out_ref.at[:, own],
            send_sem=send_sem.at[step - 1],
            recv_sem=recv_sem.at[step - 1],
            device_id={"dp": base + peer},
            device_id_type=pl.DeviceIdType.MESH,
        )
        copy.start()
        copies.append(copy)
    out_ref[:, own] = rows_ref[:, own]
    for copy in copies:
        copy.wait()


def in_vmem(count):
    return [pl.BlockSpec(memory_space=pltpu.VMEM)] * count


def params(number):
    return pltpu.CompilerParams(collective_id=number, has_side_effects=True, vmem_limit_bytes=16 << 20)


def sems(ways):
    return [pltpu.SemaphoreType.DMA((ways - 1,)), pltpu.SemaphoreType.DMA((ways - 1,))]


def mp_scatter(part, number):
    ways = lax.axis_size("mp")
    rows, width = part.shape[0], part.shape[1] // ways
    return pl.pallas_call(
        functools.partial(scatter_kernel, ways),
        out_shape=jax.ShapeDtypeStruct((rows, width), jnp.float32),
        in_specs=in_vmem(1),
        out_specs=pl.BlockSpec(memory_space=pltpu.VMEM),
        scratch_shapes=[pltpu.VMEM((ways - 1, rows, width), part.dtype)] + sems(ways),
        compiler_params=params(number),
        cost_estimate=pl.CostEstimate(flops=rows * width * 4, bytes_accessed=part.size * 4, transcendentals=0),
        name="mp_scatter",
    )(part)


def mp_gather(own, number):
    ways = lax.axis_size("mp")
    rows, width = own.shape
    return pl.pallas_call(
        functools.partial(gather_kernel, ways),
        out_shape=jax.ShapeDtypeStruct((rows, ways * width), own.dtype),
        in_specs=in_vmem(1),
        out_specs=pl.BlockSpec(memory_space=pltpu.VMEM),
        scratch_shapes=sems(ways),
        compiler_params=params(number),
        cost_estimate=pl.CostEstimate(flops=0, bytes_accessed=own.size * 10, transcendentals=0),
        name="mp_gather",
    )(own)


def mp_gather_sum(own, term, number):
    ways = lax.axis_size("mp")
    rows, width = own.shape
    return pl.pallas_call(
        functools.partial(gather_sum_kernel, ways),
        out_shape=(
            jax.ShapeDtypeStruct((rows, ways * width), own.dtype),
            jax.ShapeDtypeStruct(term.shape, term.dtype),
        ),
        in_specs=in_vmem(2),
        out_specs=tuple(in_vmem(2)),
        scratch_shapes=[pltpu.VMEM((ways - 1,) + term.shape, term.dtype)] + sems(ways) + sems(ways),
        compiler_params=params(number),
        cost_estimate=pl.CostEstimate(flops=0, bytes_accessed=own.size * 10, transcendentals=0),
        name="mp_gather_sum",
    )(own, term)


def mp_sum(term, number):
    ways = lax.axis_size("mp")
    return pl.pallas_call(
        functools.partial(sum_kernel, ways),
        out_shape=jax.ShapeDtypeStruct(term.shape, term.dtype),
        in_specs=in_vmem(1),
        out_specs=pl.BlockSpec(memory_space=pltpu.VMEM),
        scratch_shapes=[pltpu.VMEM((ways - 1,) + term.shape, term.dtype)] + sems(ways),
        compiler_params=params(number),
        cost_estimate=pl.CostEstimate(flops=0, bytes_accessed=term.size * 20, transcendentals=0),
        name="mp_sum",
    )(term)


def column_gather(block, part, plane, parts, number):
    ways = lax.axis_size("mp")
    depth = lax.axis_size("dp") // plane
    rows, width = part.shape[0], part.shape[1] // ways
    up_steps, down_steps = depth // 2, depth - 1 - depth // 2
    sem = pltpu.SemaphoreType.DMA
    return pl.pallas_call(
        functools.partial(column_kernel, ways, plane, parts),
        out_shape=(
            jax.ShapeDtypeStruct((depth,) + block.shape, block.dtype),
            jax.ShapeDtypeStruct((rows, width), jnp.float32),
        ),
        in_specs=in_vmem(2),
        out_specs=tuple(in_vmem(2)),
        scratch_shapes=[pltpu.VMEM((ways - 1, rows, width), part.dtype)]
        + sems(ways)
        + [sem((up_steps * parts,)), sem((up_steps * parts,)), sem((down_steps * parts,)), sem((down_steps * parts,))],
        compiler_params=params(number),
        name="column_gather",
    )(block, part)


def plane_exchange(rows, plane, capacity, number):
    sem = pltpu.SemaphoreType.DMA
    return pl.pallas_call(
        functools.partial(plane_kernel, plane, capacity),
        out_shape=jax.ShapeDtypeStruct(rows.shape, rows.dtype),
        in_specs=in_vmem(1),
        out_specs=pl.BlockSpec(memory_space=pltpu.VMEM),
        scratch_shapes=[sem((plane - 1,)), sem((plane - 1,))],
        compiler_params=params(number),
        name="plane_exchange",
    )(rows)


def encode_part(states, w_in, w_out):
    pre_act = jnp.dot(states, w_in, preferred_element_type=jnp.float32)
    hidden = gelu_value(pre_act).astype(jnp.bfloat16)
    return (pre_act, jnp.dot(hidden, w_out, preferred_element_type=jnp.float32).astype(jnp.bfloat16))


def decode(grad_own, pre_act, out_own, out_full, inv_norm, w_in, w_out, number):
    inv = inv_norm[:, None]
    unit_own = out_own * inv
    dot_part = jnp.sum(unit_own * grad_own, axis=1)
    grad_full, dots = mp_gather_sum(
        grad_own.astype(jnp.bfloat16), jnp.broadcast_to(dot_part[None, :], (8, dot_part.shape[0])), number
    )
    dot_all = dots[0][:, None]
    grad_out = inv * (grad_full.astype(jnp.float32) - out_full.astype(jnp.float32) * (inv * dot_all))
    grad_out_own = inv * (grad_own - unit_own * dot_all)
    contract = (((1,), (1,)), ((), ()))
    grad_hidden = lax.dot_general(
        grad_out.astype(jnp.bfloat16), w_out, contract, preferred_element_type=jnp.float32
    )
    grad_pre = (grad_hidden * gelu_slope(pre_act)).astype(jnp.bfloat16)
    partial_in = lax.dot_general(grad_pre, w_in, contract, preferred_element_type=jnp.float32)
    summed = mp_scatter(partial_in.astype(jnp.bfloat16), number + 1)
    return (summed + grad_out_own).astype(jnp.bfloat16)


def encode(states, w_in, w_out, number):
    pre_act = jnp.dot(states, w_in, preferred_element_type=jnp.float32)
    hidden = gelu_value(pre_act).astype(jnp.bfloat16)
    partial_out = jnp.dot(hidden, w_out, preferred_element_type=jnp.float32).astype(jnp.bfloat16)
    return (pre_act, own_columns(states).astype(jnp.float32) + mp_scatter(partial_out, number))


def shards(query_states, passage_states, w_in, w_out, neg_owner, neg_mask, served_rows, loss_scale):
    owners = lax.axis_size("dp")
    row_count = query_states.shape[0]
    capacity = served_rows.shape[2]
    slots = owners * capacity
    pre_pass, out_pass = encode(passage_states, w_in, w_out, 0)
    half_pass = out_pass.astype(jnp.bfloat16)
    column_width = half_pass.shape[1]

    served = served_rows[0].reshape(-1)
    served_pick = (served[:, None] == jnp.arange(row_count, dtype=jnp.int32)[None, :]).astype(jnp.bfloat16)
    plane, depth = 8, owners // 8
    block = jnp.concatenate(
        [
            half_pass,
            served.astype(jnp.bfloat16).reshape(-1, column_width),
            jnp.zeros((16 - served.shape[0] // column_width, column_width), jnp.bfloat16),
        ],
        axis=0,
    )
    pre_query, part_query = encode_part(query_states, w_in, w_out)
    column, sum_query = column_gather(block, part_query, plane, 3, 7)
    out_query = own_columns(query_states).astype(jnp.float32) + sum_query
    start = (lax.axis_index("dp") // plane) * plane * capacity
    served_here = lax.dynamic_slice(
        column,
        (0, row_count + start // column_width, lax.rem(start, column_width)),
        (depth, 1, plane * capacity),
    ).reshape(depth, plane * capacity)
    wanted = served_here.astype(jnp.int32)[:, :, None] == jnp.arange(row_count, dtype=jnp.int32)[None, None, :]
    chosen = lax.dot_general(
        wanted.astype(jnp.bfloat16),
        column[:, :row_count],
        (((2,), (1,)), ((0,), (0,))),
        preferred_element_type=jnp.float32,
    ).astype(jnp.bfloat16)
    slot_rows = plane_exchange(chosen, plane, capacity, 8).reshape(slots, column_width)
    half_query = out_query.astype(jnp.bfloat16)
    out_full = mp_gather(jnp.concatenate([half_pass, half_query], axis=0), 1)
    owner_rows = neg_owner.T
    named = owner_rows[:, :, None] == jnp.arange(owners, dtype=jnp.int32)[None, None, :]
    names = jnp.any(named, axis=0).astype(jnp.bfloat16)
    spot = jnp.arange(row_count, dtype=jnp.int32)
    earlier = (spot[None, :] < spot[:, None]).astype(jnp.bfloat16)
    before = jnp.dot(earlier, names, preferred_element_type=jnp.float32)
    slot_index = jnp.sum(jnp.where(named, before[None, :, :], 0.0), axis=2).astype(jnp.int32)
    slot_place = owner_rows * capacity + slot_index
    slot_hit = slot_place[:, :, None] == jnp.arange(slots, dtype=jnp.int32)[None, None, :]

    slot_part = lax.dot_general(half_query, slot_rows, (((1,), (1,)), ((), ())), preferred_element_type=jnp.float32)
    slot_wide = slot_rows.astype(jnp.float32)
    slot_square = jnp.sum(slot_wide * slot_wide, axis=1)
    neg_part = jnp.sum(jnp.where(slot_hit, slot_part[None, :, :], 0.0), axis=2)
    neg_square = jnp.sum(jnp.where(slot_hit, slot_square[None, None, :], 0.0), axis=2)
    pos_part = jnp.sum(half_query.astype(jnp.float32) * half_pass.astype(jnp.float32), axis=1)
    squares = jnp.stack([jnp.sum(out_pass * out_pass, axis=1), jnp.sum(out_query * out_query, axis=1)])
    extra = jnp.concatenate([pos_part[None, :], squares, jnp.zeros((5, row_count), jnp.float32)], axis=0)
    sums = mp_sum(jnp.concatenate([neg_part, neg_square, extra], axis=0), 2)
    negatives = neg_owner.shape[1]
    inv_neg = lax.rsqrt(sums[negatives : 2 * negatives] + norm_eps)
    inv_pass = lax.rsqrt(sums[2 * negatives + 1] + norm_eps)
    inv_query = lax.rsqrt(sums[2 * negatives + 2] + norm_eps)
    pos_score = sums[2 * negatives] * inv_query * inv_pass
    neg_score = sums[:negatives] * inv_query[None, :] * inv_neg
    exp_pos = jnp.exp(logit_scale * pos_score)
    exp_neg = neg_mask.T.astype(jnp.float32) * jnp.exp(logit_scale * neg_score)
    denominator = exp_pos + jnp.sum(exp_neg, axis=0)
    factor = loss_scale * logit_scale
    grad_pos = factor * (exp_pos / denominator - 1.0)
    grad_neg = factor * exp_neg / denominator[None, :]

    slot_grad = jnp.sum(jnp.where(slot_hit, (grad_neg * inv_query[None, :])[:, :, None], 0.0), axis=0)
    outgoing_grad = lax.dot_general(
        slot_grad.astype(jnp.bfloat16), half_query, (((0,), (0,)), ((), ())), preferred_element_type=jnp.float32
    ).astype(jnp.bfloat16)
    late_weight, outgoing_grad = lax.optimization_barrier((grad_neg * inv_neg, outgoing_grad))
    returned = lax.all_to_all(
        outgoing_grad.reshape(owners, capacity, column_width), "dp", split_axis=0, concat_axis=0, tiled=True
    ).reshape(slots, column_width)
    slot_weight = jnp.sum(jnp.where(slot_hit, late_weight[:, :, None], 0.0), axis=0)
    grad_query_emb = (grad_pos * inv_pass)[:, None] * out_pass + jnp.dot(
        slot_weight.astype(jnp.bfloat16), slot_rows, preferred_element_type=jnp.float32
    )
    grad_query_states = decode(
        grad_query_emb, pre_query, out_query, out_full[row_count:], inv_query, w_in, w_out, 3
    )
    returned, grad_query_states = lax.optimization_barrier((returned, grad_query_states))
    gathered_back = lax.dot_general(
        served_pick, returned, (((0,), (0,)), ((), ())), preferred_element_type=jnp.float32
    )
    grad_pass_emb = (grad_pos * inv_query)[:, None] * out_query + gathered_back
    grad_passage_states = decode(
        grad_pass_emb, pre_pass, out_pass, out_full[:row_count], inv_pass, w_in, w_out, 5
    )
    return (grad_query_states, grad_passage_states)


def solution(mesh):
    in_specs = (
        P("dp", None),
        P("dp", None),
        P(None, "mp"),
        P("mp", None),
        P("dp", None),
        P("dp", None),
        P("dp", None, None),
        P(),
    )
    out_specs = (P("dp", "mp"), P("dp", "mp"))
    return jax.shard_map(shards, mesh=mesh, in_specs=in_specs, out_specs=out_specs, check_vma=False)
```
